32 devices in a mesh: gx: 4 (over y, x), gy: 8 (over z, core).
Axes of the slice: x: 2, y: 2, z: 4, core: 2. Of those that a mesh axis runs over, the one named last changes fastest.
Arguments:
- eigvecs: float32 [24, 512, 1024], P(None, 'gx', 'gy'), may hold values from -40 to 40
- search_dir: float32 [24, 512, 1024], P(None, 'gx', 'gy'), may hold values from -3 to 3
- conduct: float32 [2, 512, 1024], P(None, 'gx', 'gy'), may hold values from 0.1 to 10
- shift: float32 [512, 1024], P('gx', 'gy'), may hold values from 0.01 to 1
- aggregate: int32 [64, 128], P('gx', 'gy'), may hold values from 0 to 127, as said below
- coarse_cols: int32 [32, 3], P(('gx', 'gy')), may hold values from 0 to 31, as said below
- coarse_vals: bfloat16 [32, 3, 128, 128], P(('gx', 'gy')), may hold values from -85 to 300, as said below
Outputs:
- precond: float32 [24, 512, 1024], P(None, 'gx', 'gy')
- gram_a: float32 [72, 72], replicated
- gram_b: float32 [72, 72], replicated
The draws below stay inside these ranges and needn't reach their ends.
Inputs may be any that keep to these rules, and one draw needn't show every extreme that they name: Within one device's tile of blocks, every aggregate id names the same number of blocks. `coarse_cols`: entry 0 of block row d is d itself; the 3 column blocks of a row are distinct. `coarse_vals`: the diagonal of each self block exceeds the sum of magnitudes of the other entries of its row.
All inputs are finite; a program needn't handle non-finite values.
Results may differ from the reference program's by a relative error of at most 0.0003.
Values may be sent and summed in bfloat16 or wider, within the bound.
A program may use at most 128 MiB of HBM per device.

```python
import math
import jax
import jax.numpy as jnp
from jax import lax

K = 24
CX = 128
CY = 128
AGG_DEV = 128
COARSE_NB = 3
COARSE_SWEEPS = 4
SMOOTH_STEPS = 3
NDEV = 32
NX = 512
NY = 1024
NC = 4096
N_GX = 4
N_GY = 8


def draw_eigvecs(key, part):
    rows = jnp.arange(NX, dtype=jnp.float32) / max(NX - 1, 1)
    rising = jnp.exp(jnp.log(3.0) * rows)[None, :, None]
    base = jnp.clip(jax.random.normal(key, (K, NX, NY), jnp.float32), -4.0, 4.0)
    return base * rising


def draw_aggregate(key, part):
    nbx = CX // 8
    nby = CY // 8
    count = nbx * nby
    tiles = N_GX * N_GY
    scores = jax.random.randint(key, (tiles, count), 0, 2 ** 20) * count + jnp.arange(count, dtype=jnp.int32)[None, :]
    order = jnp.argsort(scores, axis=1, stable=True).astype(jnp.int32)
    ids = order % AGG_DEV
    ids = ids.reshape(N_GX, N_GY, nbx, nby).transpose(0, 2, 1, 3)
    return ids.reshape(N_GX * nbx, N_GY * nby).astype(jnp.int32)


def draw_coarse_cols(key, part):
    scores = jax.random.randint(key, (NDEV, NDEV - 1), 0, 2 ** 20) * NDEV + jnp.arange(NDEV - 1, dtype=jnp.int32)[None, :]
    offsets = jnp.argsort(scores, axis=1, stable=True)[:, :COARSE_NB - 1].astype(jnp.int32) + 1
    rows = jnp.arange(NDEV, dtype=jnp.int32)[:, None]
    return jnp.concatenate([rows, (rows + offsets) % NDEV], axis=1).astype(jnp.int32)


def draw_coarse_vals(key, part):
    key_weak = jax.random.fold_in(key, 11)
    key_diag = jax.random.fold_in(key, 12)
    key_cols = jax.random.fold_in(key, 13)
    key_self = jax.random.fold_in(key, 14)
    key_mags = jax.random.fold_in(key, 15)
    shape = (NDEV, COARSE_NB, AGG_DEV, AGG_DEV)
    row_shape = (NDEV, COARSE_NB, AGG_DEV)
    weak = jnp.clip(0.0001 * jax.random.normal(key_weak, shape, jnp.float32), -0.0003, 0.0003)
    mags = jax.random.uniform(key_mags, row_shape, jnp.float32, 0.15, 0.28)
    top = jax.random.uniform(key_diag, (NDEV, AGG_DEV), jnp.float32, 120.0, 299.0)
    rows = jnp.arange(AGG_DEV, dtype=jnp.int32)[None, None, :]
    other_pick = jax.random.randint(key_cols, row_shape, 0, AGG_DEV).astype(jnp.int32)
    self_pick = ((rows + 1 + jax.random.randint(key_self, row_shape, 0, AGG_DEV - 1)) % AGG_DEV).astype(jnp.int32)
    first_row = (jnp.arange(COARSE_NB, dtype=jnp.int32) == 0)[None, :, None]
    picks = jnp.where(first_row, self_pick, other_pick)
    columns = jnp.arange(AGG_DEV, dtype=jnp.int32)[None, None, None, :]
    strong = (picks[..., None] == columns).astype(jnp.float32) * mags[..., None]
    scale_rows = top[:, None, :, None]
    off = (weak - strong) * scale_rows
    eye = jnp.eye(AGG_DEV, dtype=jnp.float32)[None, None]
    first = (jnp.arange(COARSE_NB) == 0).astype(jnp.float32)[None, :, None, None]
    return (off * (1.0 - first * eye) + first * eye * scale_rows).astype(jnp.bfloat16)


def shard_levels(stream_key, shape, shards, smallest, largest):
    loudness, own = 1.0, jax.random.fold_in(stream_key, 6)
    for dim, blocks in shards:
        steps = jnp.exp(jax.random.uniform(jax.random.fold_in(own, dim), (blocks,), jnp.float32, smallest / len(shards), largest / len(shards)))
        loudness = loudness * jnp.repeat(steps, shape[dim] // blocks).reshape([-1 if axis == dim else 1 for axis in range(len(shape))])
    return loudness


def centred(stream_key, shape, deviation, bound, pieces=(), kind=jnp.bfloat16):
    array = jax.random.normal(stream_key, shape, jnp.float32) * deviation
    if len(pieces) > 0:
        array = shard_levels(stream_key, shape, pieces, -0.22, 0.18) * array
    return jnp.clip(array, min=-bound, max=bound).astype(kind)


def setup_inputs(seed: int = 0) -> dict:
    key_of = jax.random.split(jax.random.key(seed), 8)
    return {
        "eigvecs": draw_eigvecs(jax.random.fold_in(key_of[7], 71), 0),
        "search_dir": centred(key_of[1], (K, NX, NY), 0.5, 3.0, ((1, 4), (2, 8)), jnp.float32),
        "conduct": jnp.clip(jnp.exp(math.log(10.0) - 4.6051702 * jax.random.uniform(key_of[2], (2, NX, NY), jnp.float32) ** shard_levels(key_of[2], (2, NX, NY), ((1, 4), (2, 8)), -0.2, 0.2)), 0.1, 10.0),
        "shift": jnp.clip(jnp.exp(math.log(1.0) - 4.6051702 * jax.random.uniform(key_of[3], (NX, NY), jnp.float32) ** shard_levels(key_of[3], (NX, NY), ((0, 4), (1, 8)), -0.2, 0.2)), 0.01, 1.0),
        "aggregate": draw_aggregate(jax.random.fold_in(key_of[7], 71), 0),
        "coarse_cols": draw_coarse_cols(jax.random.fold_in(key_of[7], 71), 0),
        "coarse_vals": draw_coarse_vals(jax.random.fold_in(key_of[7], 71), 0),
    }


cheb_lo = 0.3
cheb_hi = 2.0
damping = 0.6


def chebyshev(start, resid, inverse, operate, steps, update_last):
    theta = (cheb_hi + cheb_lo) / 2.0
    delta = (cheb_hi - cheb_lo) / 2.0
    sigma = theta / delta
    rho = 1.0 / sigma
    direction = inverse * resid / theta
    start = start + direction
    if steps > 1 or update_last:
        resid = resid - operate(direction)
    for step in range(1, steps):
        rho_new = 1.0 / (2.0 * sigma - rho)
        direction = (rho_new * rho) * direction + (2.0 * rho_new / delta) * (inverse * resid)
        start = start + direction
        if step < steps - 1 or update_last:
            resid = resid - operate(direction)
        rho = rho_new
    return start, resid


def inner(left, right):
    flat_l = left.reshape(left.shape[0], -1)
    flat_r = right.reshape(right.shape[0], -1)
    return lax.dot_general(flat_l, flat_r, (((1,), (1,)), ((), ())), precision=lax.Precision.HIGHEST, preferred_element_type=jnp.float32)


def reference(eigvecs, search_dir, conduct, shift, aggregate, coarse_cols, coarse_vals):
    count = eigvecs.shape[0]
    cond_x = conduct[0]
    cond_y = conduct[1]
    prev_x = jnp.pad(cond_x, ((1, 0), (0, 0)))[:-1]
    prev_y = jnp.pad(cond_y, ((0, 0), (1, 0)))[:, :-1]
    diagonal = cond_x + prev_x + cond_y + prev_y + shift
    inverse = 1.0 / diagonal

    def operate(field):
        ext = jnp.pad(field, ((0, 0), (1, 1), (1, 1)))
        return (diagonal * field - cond_x * ext[:, 2:, 1:-1] - prev_x * ext[:, :-2, 1:-1]
                - cond_y * ext[:, 1:-1, 2:] - prev_y * ext[:, 1:-1, :-2])

    image_x = operate(eigvecs)
    image_p = operate(search_dir)
    lam = jnp.sum(eigvecs * image_x, axis=(1, 2)) / jnp.sum(eigvecs * eigvecs, axis=(1, 2))
    resid = image_x - lam[:, None, None] * eigvecs

    smooth, left = chebyshev(jnp.zeros_like(resid), resid, inverse, operate, SMOOTH_STEPS, True)

    nbx_all = NX // 8
    nby_all = NY // 8
    bx = jnp.arange(nbx_all, dtype=jnp.int32)[:, None]
    by = jnp.arange(nby_all, dtype=jnp.int32)[None, :]
    owner = (bx // (CX // 8)) * N_GY + by // (CY // 8)
    unknown = (owner * AGG_DEV + aggregate).reshape(-1).astype(jnp.int32)
    blocks = left.reshape(count, nbx_all, 8, nby_all, 8).sum(axis=(2, 4)).reshape(count, -1)
    coarse_rhs = jax.ops.segment_sum(blocks.T, unknown, num_segments=NC).T

    weights = coarse_vals.astype(jnp.float32)
    ndev = weights.shape[0]
    coarse_diag = jnp.diagonal(weights[:, 0], axis1=1, axis2=2).reshape(-1)
    corr = damping * coarse_rhs / coarse_diag[None, :]
    for sweep in range(COARSE_SWEEPS - 1):
        picks = corr.reshape(count, ndev, AGG_DEV)[:, coarse_cols]
        prod = jnp.einsum("dkab,ndkb->nda", weights, picks, precision=lax.Precision.HIGHEST).reshape(count, -1)
        corr = corr + damping * (coarse_rhs - prod) / coarse_diag[None, :]

    spread = corr[:, unknown].reshape(count, nbx_all, 1, nby_all, 1)
    fine_corr = jnp.broadcast_to(spread, (count, nbx_all, 8, nby_all, 8)).reshape(count, NX, NY)
    smooth = smooth + fine_corr
    left = left - operate(fine_corr)
    precond, unused = chebyshev(smooth, left, inverse, operate, SMOOTH_STEPS, False)
    image_w = operate(precond)

    basis = [eigvecs, precond, search_dir]
    images = [image_x, image_w, image_p]
    gram_a = jnp.concatenate([jnp.concatenate([inner(s, a) for a in images], axis=1) for s in basis], axis=0)
    gram_b = jnp.concatenate([jnp.concatenate([inner(s, t) for t in basis], axis=1) for s in basis], axis=0)
    return precond, gram_a, gram_b
```

```python
import functools

import jax
import jax.numpy as jnp
from jax import lax
from jax.experimental import pallas as pl
from jax.experimental.pallas import tpu as pltpu
from jax.sharding import PartitionSpec as P

H = 8
LANES = 128
VMEM_CAP = 60 * 1024 * 1024

cheb_lo = 0.3
cheb_hi = 2.0
damping = 0.6
theta = (cheb_hi + cheb_lo) / 2.0
delta = (cheb_hi - cheb_lo) / 2.0
sigma = theta / delta
RHO0 = 1.0 / sigma
RHO1 = 1.0 / (2.0 * sigma - RHO0)
RHO2 = 1.0 / (2.0 * sigma - RHO1)
CHEB = ((RHO1 * RHO0, 2.0 * RHO1 / delta), (RHO2 * RHO1, 2.0 * RHO2 / delta))

CONTRACT_LAST = (((1,), (1,)), ((), ()))
CXS, PXS, CYS, PYS, DIA, INV, AGG = range(7)
f32 = jnp.float32


def split2(value):
    high = value.astype(jnp.bfloat16)
    low = (value - high.astype(f32)).astype(jnp.bfloat16)
    return high, low


def turn(value, by):
    by = by % LANES
    return pltpu.roll(value, by, 1) if by else value


def dot_last(a, b):
    return lax.dot_general(a, b, CONTRACT_LAST, preferred_element_type=f32)


def remote(src, dst, send, recv, peer):
    return pltpu.make_async_remote_copy(src_ref=src, dst_ref=dst, send_sem=send, recv_sem=recv,
                                        device_id=peer, device_id_type=pl.DeviceIdType.MESH)


def kernel(ngx, ngy, rows, x2, x3, p2, cond, shift, agg, cols, vals, out, ga_ref, gb_ref,
           xr, pr, C, top, bot, pb, toe, tow, pc, wb, eb, wc, ec, nwb, neb, swb, seb, nwc, nec, swc, sec,
           XW, B, S, D1, D2, SM, AX, TP, CO, n1, n2, vv, G0, G1, G2, RS, rhs_ref, near, FA, FR, FL,
           xw_out, t1, u1, u2, u3, part, dloc, hs, hr, ns1, nr1, ns2, nr2, gs1, gr1, gs2, gr2, as_, ar_,
           es1, er1, es2, er2, es3, er3):
    count = x3.shape[0]
    ext = rows + 2 * H
    ng = count // H
    quarter = rows // 4
    i, j = lax.axis_index("gx"), lax.axis_index("gy")
    me = i * ngy + j
    peers_y = [(i, lax.rem(j + o, ngy)) for o in range(1, ngy)]
    peers_x = [(lax.rem(i + o, ngx), j) for o in range(1, ngx)]
    steps = [(s, t) for s in range(3) for t in range(3) if (s, t) != (1, 1)]

    def wrapped(dx, dy):
        return (lax.rem(i + dx + ngx, ngx), lax.rem(j + dy + ngy, ngy))

    lane = lax.broadcasted_iota(jnp.int32, (H, LANES), 1)
    LL = lax.rem(lane + H, LANES)
    in_a = lax.rem(LL, 16) < 8
    win = [LL // 16 == g for g in range(ng)]
    in_win = LL < 16 * ng
    at_r = [lane == (16 * g - 1) % LANES for g in range(ng)]
    at_l = [lane == 16 * g for g in range(ng)]

    local = [pltpu.make_async_copy(x2, xr, dloc.at[0]), pltpu.make_async_copy(p2, pr, dloc.at[1]),
             pltpu.make_async_copy(cond, C.at[0:2, H:H + rows], dloc.at[2]),
             pltpu.make_async_copy(shift, C.at[2, H:H + rows], dloc.at[3]),
             pltpu.make_async_copy(vals, vv, dloc.at[4])]
    for copy in local:
        copy.start()

    diagonal = [wrapped(dx, dy) for dx in (-1, 1) for dy in (-1, 1)]
    greeted = peers_y + peers_x + diagonal
    barrier = pltpu.get_barrier_semaphore()
    for peer in greeted:
        pl.semaphore_signal(barrier, inc=1, device_id=peer, device_id_type=pl.DeviceIdType.MESH)

    expand = jnp.where(lax.broadcasted_iota(jnp.int32, (agg.shape[1], LANES), 1) // H
                       == lax.broadcasted_iota(jnp.int32, (agg.shape[1], LANES), 0), 1.0, 0.0).astype(jnp.bfloat16)
    ids = jnp.dot(agg[...].astype(f32).astype(jnp.bfloat16), expand, preferred_element_type=f32)
    for b in range(rows // H):
        C[3, H + b * H:2 * H + b * H, :] = jnp.broadcast_to(ids[b:b + 1, :], (H, LANES))

    def raw(ref, g, r, stride):
        return ref[pl.ds(g * H * stride + r, H, stride), :]

    local[0].wait()
    local[1].wait()

    def pack(r, _):
        east = west = None
        for q in reversed(range(4)):
            row = q * quarter + r
            m = [turn(raw(xr, g, row, rows), 16 * g) for g in range(ng)]
            for g in range(ng):
                XW[H + row, g * H:(g + 1) * H, :] = m[g]
            both = m[ng - 1]
            for g in range(ng - 1):
                both = jnp.where(win[g], m[g], both)
            fe = turn(both, H * (q % 2) + 48 * (q // 2))
            fw = turn(both, -H * (q % 2) + 48 * (q // 2))
            if q == 3:
                east, west = fe, fw
            else:
                low = (LL < 48) if q < 2 else (LL < 96)
                ea = in_a if q % 2 == 0 else ~in_a
                wa = ~in_a if q % 2 == 0 else in_a
                east = jnp.where(low & ea, fe, east)
                west = jnp.where(low & wa, fw, west)
        for q in range(4):
            for g in range(ng):
                to = 88 + 4 * g + q
                west = jnp.where(lane == to, turn(raw(pr, g, q * quarter + r, rows), to), west)
        toe[r] = east
        tow[r] = west
        return 0

    lax.fori_loop(0, quarter, pack, 0)
    for g in range(ng):
        part[g * H:(g + 1) * H, :] = raw(pr, g, 0, rows)
    local[2].wait()
    local[3].wait()
    half = rows // 2
    lane_h = lax.broadcasted_iota(jnp.int32, (half, LANES), 1)
    LLh = lax.rem(lane_h + H, LANES)

    def coef_pack(lo):
        total = C[3, H + lo:H + lo + half, :]
        total = turn(total, 48)
        for n in range(3):
            total = jnp.where(LLh // 16 == n, turn(C[n, H + lo:H + lo + half, :], 16 * n), total)
        return total

    pc[...] = jnp.where(LLh < 64, coef_pack(0), turn(coef_pack(half), 64))
    pl.semaphore_wait(barrier, len(greeted))

    last = quarter - H
    moves = {
        (-1, 0): [(x3.at[:, 0:H], bot), (C.at[:, H:2 * H], C.at[:, H + rows:ext]), (part, pb)],
        (1, 0): [(x3.at[:, rows - H:rows], top), (C.at[:, rows:rows + H], C.at[:, 0:H])],
        (0, 1): [(toe, wb), (pc, wc)],
        (0, -1): [(tow, eb), (pc, ec)],
        (-1, 1): [(toe.at[0:H], swb), (pc.at[0:H], swc)],
        (-1, -1): [(tow.at[0:H], seb), (pc.at[0:H], sec)],
        (1, 1): [(toe.at[last:quarter], nwb), (pc.at[half - H:half], nwc)],
        (1, -1): [(tow.at[last:quarter], neb), (pc.at[half - H:half], nec)],
    }

    def exists(dx, dy):
        return (i + dx >= 0) & (i + dx < ngx) & (j + dy >= 0) & (j + dy < ngy)

    def copies_of(d):
        base = 3 * list(moves).index(d)
        return [remote(src, dst, hs.at[base + n], hr.at[base + n], (i + d[0], j + d[1]))
                for n, (src, dst) in enumerate(moves[d])]

    for d in moves:
        @pl.when(exists(*d))
        def _(d=d):
            for copy in copies_of(d):
                copy.start()

        @pl.when(jnp.logical_not(exists(-d[0], -d[1])))
        def _(d=d):
            for _, dst in moves[d]:
                dst[...] = jnp.zeros(dst.shape, dst.dtype)

    for ref in (S,):
        for row in (0, 1, ext - 2, ext - 1):
            ref[row] = jnp.zeros(ref.shape[1:], f32)

    for d in moves:
        @pl.when(exists(-d[0], -d[1]))
        def _(d=d):
            for copy in copies_of(d):
                copy.wait_recv()

    for ref, at in ((top, 0), (bot, H + rows)):
        flat = ref.reshape(count * H, LANES)
        for r in range(H):
            for g in range(ng):
                XW[at + r, g * H:(g + 1) * H, :] = turn(raw(flat, g, r, H), 16 * g)

    def edge(w, e, q):
        w = turn(w, -(H * (q % 2) + 48 * (q // 2)))
        e = turn(e, H * (q % 2) - 48 * (q // 2))
        return jnp.where(in_win, jnp.where(in_a, w, e), 0.0)

    at_e = slice(ng * H, (ng + 1) * H)

    def unpack(r, _):
        for q in range(4):
            XW[H + q * quarter + r, at_e, :] = edge(wb[r], eb[r], q)
        return 0

    lax.fori_loop(0, quarter, unpack, 0)
    for r in range(H):
        XW[r, at_e, :] = edge(nwb[r], neb[r], 3)
        XW[H + rows + r, at_e, :] = edge(swb[r], seb[r], 0)

    def masks(number):
        ln = lax.broadcasted_iota(jnp.int32, (number, LANES), 1)
        return ln, lax.rem(ln + H, LANES)

    def joined(w, e):
        _, l2 = masks(w.shape[0])
        return jnp.where(lax.rem(l2, 16) < 8, w, e)

    side = joined(wc[...], ec[...])
    wide = jnp.concatenate([turn(joined(nwc[...], nec[...]), 64), side, turn(side, 64),
                            joined(swc[...], sec[...])], axis=0)
    lnx, llx = masks(ext)

    def fields(n):
        m = C[n]
        res = [turn(m, 16 * g) for g in range(ng)]
        e = jnp.zeros_like(wide)
        for g in range(ng):
            e = jnp.where(llx // 16 == g, turn(wide, 16 * (g - n)), e)
        return res + [e]

    def lefts(v, ml):
        l = [turn(a, 1) for a in v]
        e = l[ng]
        for g in range(ng):
            e = jnp.where(ml[g], l[g], e)
        return [jnp.where(ml[g], l[ng], l[g]) for g in range(ng)] + [e]

    def rights(v, mr):
        l = [turn(a, LANES - 1) for a in v]
        e = l[ng]
        for g in range(ng):
            e = jnp.where(mr[g], l[g], e)
        return [jnp.where(mr[g], l[ng], l[g]) for g in range(ng)] + [e]

    cx, cy, sh, ag = fields(0), fields(1), fields(2), fields(3)
    mlx = [lnx == 16 * g for g in range(ng)]
    py = lefts(cy, mlx)
    for g in range(ng + 1):
        px = pltpu.roll(cx[g], 1, 0)
        diag = cx[g] + px + cy[g] + py[g] + sh[g]
        inside = sh[g] > 0.0
        inv = jnp.where(inside, 1.0 / jnp.where(inside, diag, 1.0), 0.0)
        CO[CXS, g] = inv * cx[g]
        CO[PXS, g] = inv * px
        CO[CYS, g] = inv * cy[g]
        CO[PYS, g] = inv * py[g]
        CO[DIA, g] = diag
        CO[INV, g] = inv
        CO[AGG, g] = ag[g]

    def coef(n, g, r):
        return jnp.broadcast_to(CO[n, g, pl.ds(r, 1), :], (H, LANES))

    every = range(ng + 1)
    main = range(ng)

    def get(ref, r, groups=every):
        return [ref[r, g * H:(g + 1) * H, :] for g in groups]

    def put(ref, r, v):
        for g, a in enumerate(v):
            ref[r, g * H:(g + 1) * H, :] = a

    def spreadout(r, vm, vc, vp):
        rt, lf = rights(vc, at_r), lefts(vc, at_l)
        return [coef(CXS, g, r) * vp[g] + coef(PXS, g, r) * vm[g]
                + coef(CYS, g, r) * rt[g] + coef(PYS, g, r) * lf[g] for g in every]

    def march(make, finish, first, number, unroll):
        def body(n, carry):
            vm, vc = carry
            for k in range(unroll):
                r = first + 1 + n * unroll + k
                vp = make(r + 1, k)
                finish(r, vc, spreadout(r, vm, vc, vp))
                vm, vc = vc, vp
            return vm, vc
        lax.fori_loop(0, number // unroll, body, (make(first, None), make(first + 1, None)))

    def fin_image(r, vc, t):
        put(B, r, [vc[g] - t[g] for g in every])

    march(lambda r, k: get(XW, r), fin_image, 0, ext - 2, 2)

    def ratio(n, carry):
        num, den = carry
        num, den = list(num), list(den)
        for k in range(4):
            r = H + n * 4 + k
            for g in main:
                xv = XW[r, g * H:(g + 1) * H, :]
                num[g] = num[g] + xv * (coef(DIA, g, r) * B[r, g * H:(g + 1) * H, :])
                den[g] = den[g] + xv * xv
        return tuple(num), tuple(den)

    zero = jnp.zeros((H, LANES), f32)
    num, den = lax.fori_loop(0, rows // 4, ratio, ((zero,) * ng, (zero,) * ng))
    nd = zero
    for g in main:
        nd = jnp.where(lane == 2 * g, jnp.sum(num[g], axis=1, keepdims=True), nd)
        nd = jnp.where(lane == 2 * g + 1, jnp.sum(den[g], axis=1, keepdims=True), nd)

    def summed(slots, number):
        total = slots[0]
        for n in range(1, number):
            total = total + slots[n]
        return total

    def begin(copies):
        for copy in copies:
            copy.start()
        return copies

    def finish_all(copies):
        for copy in copies:
            copy.wait()

    n1[j] = nd
    c1 = begin([remote(n1.at[j], n1.at[j], ns1.at[n], nr1.at[n], p) for n, p in enumerate(peers_y)])

    def forward(r, _):
        for q in range(4):
            row = q * quarter + r
            for g in main:
                pv = raw(pr, g, row, rows)
                nxt = turn(eb[r], LANES - 1 - (88 + 4 * g + q))
                rt = jnp.where(lane == LANES - 1, nxt, turn(pv, LANES - 1))
                below = raw(pr, g, jnp.minimum(row + 1, rows - 1), rows)
                below = jnp.where(row == rows - 1, pb[g * H:(g + 1) * H, :], below)
                TP[row, g * H:(g + 1) * H, :] = coef(DIA, 0, H + row) * (
                    0.5 * pv - coef(CXS, 0, H + row) * below - coef(CYS, 0, H + row) * rt)
        return 0

    lax.fori_loop(0, quarter, forward, 0)
    finish_all(c1)
    n2[i] = summed(n1, ngy)
    c1 = begin([remote(n2.at[i], n2.at[i], ns2.at[n], nr2.at[n], p) for n, p in enumerate(peers_x)])

    def image_rows(n, _):
        for k in range(4):
            r = n * 4 + k
            for g in main:
                AX[r, g * H:(g + 1) * H, :] = turn(
                    coef(DIA, g, H + r) * B[H + r, g * H:(g + 1) * H, :], -16 * g)
        return 0

    lax.fori_loop(0, rows // 4, image_rows, 0)
    finish_all(c1)
    nd = summed(n2, ngx)
    lam = []
    for g in main:
        a = jnp.sum(jnp.where(lane == 2 * g, nd, 0.0), axis=1, keepdims=True)
        b = jnp.sum(jnp.where(lane == 2 * g + 1, nd, 0.0), axis=1, keepdims=True)
        lam.append(jnp.broadcast_to(a / b, (H, LANES)))
    lam_e = lam[ng - 1]
    for g in range(ng - 1):
        lam_e = jnp.where(win[g], lam[g], lam_e)
    lam = lam + [lam_e]

    def make1(r, k):
        b, xv = get(B, r), get(XW, r)
        d = [(b[g] - lam[g] * (coef(INV, g, r) * xv[g])) * (1.0 / theta) for g in every]
        put(D1, r, d)
        return d

    def fin1(r, d, t):
        put(S, r, [(theta - 1.0) * d[g] + t[g] for g in every])

    def make2(r, k):
        d, s = get(D1, r), get(S, r)
        d = [CHEB[0][0] * d[g] + CHEB[0][1] * s[g] for g in every]
        put(D2, r, d)
        return d

    def fin_s(r, d, t):
        s = get(S, r)
        put(S, r, [s[g] - d[g] + t[g] for g in every])

    def make3(r, k):
        d1, d2, s = get(D1, r), get(D2, r), get(S, r)
        d = [CHEB[1][0] * d2[g] + CHEB[1][1] * s[g] for g in every]
        put(SM, r, [d1[g] + d2[g] + d[g] for g in every])
        return d

    march(make1, fin1, 1, rows + 12, 4)
    march(make2, fin_s, 1, rows + 12, 4)
    march(make3, fin_s, 3, rows + 8, 4)

    groups = near.shape[2]
    per = 2
    ids_t = lax.broadcasted_iota(jnp.int32, (groups, LANES), 0)

    def block_sum(b, _):
        for g in main:
            total = None
            for k in range(H):
                r = H + b * H + k
                term = coef(DIA, g, r) * S[r, g * H:(g + 1) * H, :]
                total = term if total is None else total + term
            RS[b, g * H:(g + 1) * H, :] = turn(total, -16 * g)
        return 0

    lax.fori_loop(0, rows // H, block_sum, 0)

    def gathered(b, total):
        parts, hots = [], []
        for k in range(per):
            parts.append(RS[b * per + k])
            own = CO[AGG, 0, pl.ds(H + (b * per + k) * H, 1), :].astype(jnp.int32)
            hots.append(jnp.where(ids_t == own, 1.0, 0.0).astype(jnp.bfloat16))
        high, low = split2(jnp.concatenate(parts, axis=1))
        return total + dot_last(jnp.concatenate([high, low], axis=0), jnp.concatenate(hots, axis=1))

    total = lax.fori_loop(0, rows // H // per, gathered, jnp.zeros((2 * count, groups), f32))
    rhs = total[:count] + total[count:]
    rhs_ref[...] = rhs

    local[4].wait()
    eye = (lax.broadcasted_iota(jnp.int32, (groups, groups), 0)
           == lax.broadcasted_iota(jnp.int32, (groups, groups), 1))
    dc = jnp.sum(jnp.where(eye, vv[0:groups].astype(f32), 0.0), axis=0, keepdims=True)
    factor = damping / dc
    e = rhs * factor

    def gram_early(lo, hi, total):
        def body(n, total):
            halves = []
            for k in range(2):
                r = 2 * n + k
                halves.append(jnp.concatenate(
                    [raw(xr, g, r, rows) for g in main] + [raw(pr, g, r, rows) for g in main]
                    + [AX[r], TP[r]], axis=0))
            high, low = split2(jnp.concatenate(halves, axis=1))
            lhs = jnp.concatenate([high[:2 * count], low[:2 * count]], axis=0)
            return total + dot_last(lhs, jnp.concatenate([high, low], axis=0))
        return lax.fori_loop(lo, hi, body, total)

    early = jnp.zeros((4 * count, 8 * count), f32)
    tiles = 2 * count // H

    for sweep in range(3):
        buf = (G0, G1, G2)[sweep]
        buf[me] = e
        cs = begin([remote(buf.at[me], buf.at[me], gs1.at[sweep, n], gr1.at[sweep, n], p)
                    for n, p in enumerate(peers_y)])
        if sweep == 0:
            early = gram_early(0, rows // 4, early)
        finish_all(cs)
        line = buf.at[pl.ds(i * ngy, ngy)]
        cs = begin([remote(line, line, gs2.at[sweep, n], gr2.at[sweep, n], p)
                    for n, p in enumerate(peers_x)])
        if sweep == 0:
            early = gram_early(rows // 4, rows // 2, early)
        own = dot_last(jnp.concatenate(split2(e), axis=0), vv[0:groups])
        finish_all(cs)
        picks = jnp.concatenate([buf[cols[0, 1]], buf[cols[0, 2]]], axis=1)
        weights = jnp.concatenate([vv[groups:2 * groups], vv[2 * groups:3 * groups]], axis=1)
        own = own + dot_last(jnp.concatenate(split2(picks), axis=0), weights)
        e = e + factor * (rhs_ref[...] - own[:count] - own[count:])

    near[4] = e
    cs = begin([remote(near.at[4], near.at[3 * s + t], as_.at[n], ar_.at[n], wrapped(1 - s, 1 - t))
                for n, (s, t) in enumerate(steps)])
    finish_all(cs)

    def spread(b, _):
        s = jnp.where(b == 0, 0, jnp.where(b == ext // H - 1, 2, 1))
        res = []
        for g in main:
            idx = coef(AGG, g, b * H).astype(jnp.int32)
            own = jnp.take_along_axis(near[3 * s + 1, g * H:(g + 1) * H, :], idx, axis=1)
            res.append(jnp.where(coef(INV, g, b * H) > 0.0, own, 0.0))
        idx = coef(AGG, ng, b * H).astype(jnp.int32)
        ev = jnp.zeros((H, LANES), f32)
        for g in main:
            lf = jnp.take_along_axis(near[3 * s, g * H:(g + 1) * H, :], idx, axis=1)
            rt = jnp.take_along_axis(near[3 * s + 2, g * H:(g + 1) * H, :], idx, axis=1)
            ev = jnp.where(win[g], jnp.where(in_a, lf, rt), ev)
        res.append(jnp.where(coef(INV, ng, b * H) > 0.0, ev, 0.0))
        put(FA, b, res)
        put(FR, b, rights(res, at_r))
        put(FL, b, lefts(res, at_l))
        return 0

    lax.fori_loop(0, ext // H, spread, 0)

    def make4(r, k):
        b = r // H
        f, fr, fl = get(FA, b), get(FR, b), get(FL, b)
        up = get(FA, (r + 1) // H) if k == 3 else f
        dn = get(FA, (r - 1) // H) if k == 0 else f
        s, x = get(S, r), get(SM, r)
        d, nx = [], []
        for g in every:
            v = s[g] - f[g] + (coef(CXS, g, r) * up[g] + coef(PXS, g, r) * dn[g]
                               + coef(CYS, g, r) * fr[g] + coef(PYS, g, r) * fl[g])
            v = v * (1.0 / theta)
            d.append(v)
            nx.append(x[g] + f[g] + v)
        put(D1, r, d)
        put(SM, r, nx)
        return d

    def make5(r, k):
        d, s, x = get(D1, r), get(S, r), get(SM, r)
        d = [CHEB[0][0] * d[g] + CHEB[0][1] * s[g] for g in every]
        put(D2, r, d)
        put(SM, r, [x[g] + d[g] for g in every])
        return d

    def make6(r, k):
        d, s, x = get(D2, r), get(S, r), get(SM, r)
        return [x[g] + (CHEB[1][0] * d[g] + CHEB[1][1] * s[g]) for g in every]

    W, AW = D1, B

    def fin6(r, w, t):
        for g in main:
            v = turn(w[g], -16 * g)
            W[r, g * H:(g + 1) * H, :] = v
            xw_out[pl.ds(g * H * rows + r - H, H, rows), :] = v
            AW[r, g * H:(g + 1) * H, :] = turn(coef(DIA, g, r) * (w[g] - t[g]), -16 * g)

    march(make4, fin1, 2, rows + 8, 4)
    march(make5, fin_s, 5, rows + 4, 4)

    march(make6, fin6, 7, rows, 4)
    store = pltpu.make_async_copy(xw_out, out, dloc.at[5])
    store.start()

    def gram_late(n, total):
        halves = []
        for k in range(2):
            r = 2 * n + k
            halves.append(jnp.concatenate(
                [raw(xr, g, r, rows) for g in main]
                + [W[H + r, 0:count, :]] + [raw(pr, g, r, rows) for g in main]
                + [W[H + r, 0:count, :], AW[H + r, 0:count, :]], axis=0))
        both = jnp.concatenate(halves, axis=1)
        high, low = split2(both)
        lhs = jnp.concatenate([high[3 * count:], low[3 * count:]], axis=0)
        rhs_ = jnp.concatenate([high[:3 * count], low[:3 * count]], axis=0)
        return total + dot_last(lhs, rhs_)

    late = lax.fori_loop(0, rows // 2, gram_late, jnp.zeros((4 * count, 6 * count), f32))

    def folded(total, width):
        total = total[:2 * count] + total[2 * count:]
        total = total[:, :width] + total[:, width:]
        return jnp.concatenate([total, jnp.zeros((2 * count, LANES - width), f32)], axis=1)

    early = folded(early, 4 * count)
    late = folded(late, 3 * count)
    for t in range(tiles):
        t1[t, 0] = early[t * H:(t + 1) * H]
        t1[t, 1] = late[t * H:(t + 1) * H]

    def each_owner(act):
        for t in range(tiles):
            @pl.when(j != t)
            def _(t=t):
                act(t)

    each_owner(lambda t: remote(t1.at[t], u1.at[j], es1.at[t], er1.at[j], (i, t)).start())

    @pl.when(j < tiles)
    def _():
        u1[j] = t1[j]
        for o in range(1, ngy):
            src = lax.rem(j + o, ngy)
            remote(t1.at[0], u1.at[src], es1.at[0], er1.at[src], (i, src)).wait_recv()
        u2[i] = summed(u1, ngy)
        cx_ = begin([remote(u2.at[i], u2.at[i], es2.at[n], er2.at[n], p) for n, p in enumerate(peers_x)])
        finish_all(cx_)
        u3[j] = summed(u2, ngx)
        for o in range(1, ngy):
            remote(u3.at[j], u3.at[j], es3.at[o], er3.at[j], (i, lax.rem(j + o, ngy))).start()
        for o in range(1, ngy):
            remote(u3.at[j], u3.at[j], es3.at[o], er3.at[j], (i, lax.rem(j + o, ngy))).wait_send()

    each_owner(lambda t: remote(t1.at[t], u1.at[j], es1.at[t], er1.at[j], (i, t)).wait_send())
    each_owner(lambda t: remote(u3.at[t], u3.at[t], es3.at[0], er3.at[t], (i, t)).wait_recv())

    E = jnp.concatenate([u3[t, 0] for t in range(tiles)], axis=0)
    L = jnp.concatenate([u3[t, 1] for t in range(tiles)], axis=0)
    c = count
    pad = jnp.zeros((LANES - 2 * c, LANES), f32)
    ET = jnp.concatenate([E, pad], axis=0).T
    LT = jnp.concatenate([L, pad], axis=0).T

    def cat(blocks):
        return jnp.concatenate([jnp.concatenate(line, axis=1) for line in blocks], axis=0)

    gb_ref[...] = cat([[E[0:c, 0:c], LT[0:c, 0:c], E[0:c, c:2 * c]],
                       [L[0:c, 0:c], L[0:c, c:2 * c], L[0:c, 2 * c:3 * c]],
                       [E[c:2 * c, 0:c], LT[2 * c:3 * c, 0:c], E[c:2 * c, c:2 * c]]])
    ga_ref[...] = cat([[E[0:c, 2 * c:3 * c], LT[0:c, c:2 * c], ET[2 * c:3 * c, c:2 * c]],
                       [L[c:2 * c, 0:c], L[c:2 * c, c:2 * c], L[c:2 * c, 2 * c:3 * c]],
                       [E[c:2 * c, 2 * c:3 * c], LT[2 * c:3 * c, c:2 * c],
                        E[c:2 * c, 3 * c:4 * c] + ET[3 * c:4 * c, c:2 * c]]])
    store.wait()
    for d in moves:
        @pl.when(exists(*d))
        def _(d=d):
            for copy in copies_of(d):
                copy.wait_send()


def per_device(eigvecs, search_dir, conduct, shift, aggregate, coarse_cols, coarse_vals):
    count, rows, width = eigvecs.shape
    groups = coarse_vals.shape[2]
    ngx, ngy = lax.axis_size("gx"), lax.axis_size("gy")
    ext = rows + 2 * H
    ng = count // H
    quarter, half = rows // 4, rows // 2
    lines = (ng + 1) * H
    tiles = 2 * count // H
    dma = pltpu.SemaphoreType.DMA
    v = pltpu.VMEM

    def fl(*shape):
        return v(shape, f32)

    scratch = [
        fl(count * rows, width), fl(count * rows, width), fl(4, ext, width),
        fl(count, H, width), fl(count, H, width), fl(count, width),
        fl(quarter, H, LANES), fl(quarter, H, LANES), fl(half, LANES),
        fl(quarter, H, LANES), fl(quarter, H, LANES), fl(half, LANES), fl(half, LANES),
        fl(H, H, LANES), fl(H, H, LANES), fl(H, H, LANES), fl(H, H, LANES),
        fl(H, LANES), fl(H, LANES), fl(H, LANES), fl(H, LANES),
        fl(ext, lines, LANES), fl(ext, lines, LANES), fl(ext, lines, LANES), fl(ext, lines, LANES),
        fl(ext, lines, LANES), fl(ext, lines, LANES),
        fl(rows, count, LANES), fl(rows, count, LANES),
        fl(7, ng + 1, ext, LANES),
        fl(ngy, H, LANES), fl(ngx, H, LANES),
        v((3 * groups, groups), jnp.bfloat16),
        fl(ngx * ngy, count, groups), fl(ngx * ngy, count, groups), fl(ngx * ngy, count, groups),
        fl(rows // H, count, LANES), fl(count, groups),
        fl(9, count, groups),
        fl(ext // H, lines, LANES), fl(ext // H, lines, LANES), fl(ext // H, lines, LANES),
        fl(count * rows, width), fl(tiles, 2, H, LANES),
        fl(ngy, 2, H, LANES), fl(ngx, 2, H, LANES), fl(ngy, 2, H, LANES),
        fl(count, LANES),
        dma((6,)), dma((24,)), dma((24,)),
        dma((ngy - 1,)), dma((ngy - 1,)), dma((ngx - 1,)), dma((ngx - 1,)),
        dma((3, ngy - 1)), dma((3, ngy - 1)), dma((3, ngx - 1)), dma((3, ngx - 1)),
        dma((8,)), dma((8,)),
        dma((tiles,)), dma((ngy,)), dma((ngx - 1,)), dma((ngx - 1,)), dma((ngy,)), dma((ngy,)),
    ]
    anyspace = pl.BlockSpec(memory_space=pl.ANY)
    vmem = pl.BlockSpec(memory_space=pltpu.VMEM)
    smem = pl.BlockSpec(memory_space=pltpu.SMEM)
    size = 3 * count
    out, ga, gb = pl.pallas_call(
        functools.partial(kernel, ngx, ngy, rows),
        out_shape=[jax.ShapeDtypeStruct((count * rows, width), f32),
                   jax.ShapeDtypeStruct((size, size), f32), jax.ShapeDtypeStruct((size, size), f32)],
        in_specs=[anyspace, anyspace, anyspace, anyspace, anyspace, vmem, smem, anyspace],
        out_specs=[anyspace, vmem, vmem],
        scratch_shapes=scratch,
        compiler_params=pltpu.CompilerParams(vmem_limit_bytes=VMEM_CAP, collective_id=0, has_side_effects=True),
        name="step",
    )(eigvecs.reshape(count * rows, width), eigvecs, search_dir.reshape(count * rows, width), conduct, shift,
      aggregate, coarse_cols, coarse_vals.reshape(-1, groups))
    return out.reshape(count, rows, width), ga, gb


def solution(mesh):
    placed = (
        P(None, "gx", "gy"),
        P(None, "gx", "gy"),
        P(None, "gx", "gy"),
        P("gx", "gy"),
        P("gx", "gy"),
        P(("gx", "gy"), None),
        P(("gx", "gy"), None, None, None),
    )
    return jax.shard_map(
        per_device,
        mesh=mesh,
        in_specs=placed,
        out_specs=(P(None, "gx", "gy"), P(), P()),
        check_vma=False,
    )
```

```python
import functools

import jax
import jax.numpy as jnp
from jax import lax
from jax.experimental import pallas as pl
from jax.experimental.pallas import tpu as pltpu
from jax.sharding import PartitionSpec as P

H = 8
LANES = 128
VMEM_CAP = 60 * 1024 * 1024

cheb_lo = 0.3
cheb_hi = 2.0
damping = 0.6
theta = (cheb_hi + cheb_lo) / 2.0
delta = (cheb_hi - cheb_lo) / 2.0
sigma = theta / delta
RHO0 = 1.0 / sigma
RHO1 = 1.0 / (2.0 * sigma - RHO0)
RHO2 = 1.0 / (2.0 * sigma - RHO1)
CHEB = ((RHO1 * RHO0, 2.0 * RHO1 / delta), (RHO2 * RHO1, 2.0 * RHO2 / delta))

CONTRACT_LAST = (((1,), (1,)), ((), ()))
CXS, PXS, CYS, PYS, DIA, INV, AGG = range(7)
f32 = jnp.float32


def loop(number, body, carry, unroll):
    def several(n, carry):
        for k in range(unroll):
            carry = body(n * unroll + k, carry)
        return carry
    return lax.fori_loop(0, number // unroll, several, carry)


def split2(value):
    high = value.astype(jnp.bfloat16)
    low = (value - high.astype(f32)).astype(jnp.bfloat16)
    return high, low


def turn(value, by):
    by = by % LANES
    return pltpu.roll(value, by, 1) if by else value


def dot_last(a, b):
    return lax.dot_general(a, b, CONTRACT_LAST, preferred_element_type=f32)


def remote(src, dst, send, recv, peer):
    return pltpu.make_async_remote_copy(src_ref=src, dst_ref=dst, send_sem=send, recv_sem=recv,
                                        device_id=peer, device_id_type=pl.DeviceIdType.MESH)


def kernel(ngx, ngy, rows, x2, x3, p2, cond, shift, agg, cols, vals, out, ga_ref, gb_ref,
           xr, pr, C, top, bot, pb, toe, tow, pc, wb, eb, wc, ec, nwb, neb, swb, seb, nwc, nec, swc, sec,
           XW, B, S, D1, D2, SM, AX, TP, CO, n1, n2, VA, CI, SC, G0, RS, near, FA, FR, FL,
           xw_out, t1, u1, u2, u3, part, dloc, hs, hr, ns1, nr1, ns2, nr2, gs1, gr1, gs2, gr2, as_, ar_,
           es1, er1, es2, er2, es3, er3, vs, vr):
    count = x3.shape[0]
    ext = rows + 2 * H
    ng = count // H
    quarter = rows // 4
    i, j = lax.axis_index("gx"), lax.axis_index("gy")
    me = i * ngy + j
    nz = ngy // 2
    z, c = j // 2, lax.rem(j, 2)
    partner = (i, j + 1 - 2 * c)
    peers_z = [(i, lax.rem(z + o, nz) * 2 + c) for o in range(1, nz)]
    peers_y = [(i, lax.rem(j + o, ngy)) for o in range(1, ngy)]
    peers_x = [(lax.rem(i + o, ngx), j) for o in range(1, ngx)]
    steps = [(s, t) for s in range(3) for t in range(3) if (s, t) != (1, 1)]

    def wrapped(dx, dy):
        return (lax.rem(i + dx + ngx, ngx), lax.rem(j + dy + ngy, ngy))

    lane = lax.broadcasted_iota(jnp.int32, (H, LANES), 1)
    LL = lax.rem(lane + H, LANES)
    in_a = lax.rem(LL, 16) < 8
    win = [LL // 16 == g for g in range(ng)]
    in_win = LL < 16 * ng
    at_r = [lane == (16 * g - 1) % LANES for g in range(ng)]
    at_l = [lane == 16 * g for g in range(ng)]

    local = [pltpu.make_async_copy(x2, xr, dloc.at[0]), pltpu.make_async_copy(p2, pr, dloc.at[1]),
             pltpu.make_async_copy(cond, C.at[0:2, H:H + rows], dloc.at[2]),
             pltpu.make_async_copy(shift, C.at[2, H:H + rows], dloc.at[3]),
             pltpu.make_async_copy(vals, VA.at[i, z, c], dloc.at[4])]
    for copy in local:
        copy.start()

    diagonal = [wrapped(dx, dy) for dx in (-1, 1) for dy in (-1, 1)]
    greeted = peers_y + peers_x + diagonal
    barrier = pltpu.get_barrier_semaphore()
    for peer in greeted:
        pl.semaphore_signal(barrier, inc=1, device_id=peer, device_id_type=pl.DeviceIdType.MESH)

    expand = jnp.where(lax.broadcasted_iota(jnp.int32, (agg.shape[1], LANES), 1) // H
                       == lax.broadcasted_iota(jnp.int32, (agg.shape[1], LANES), 0), 1.0, 0.0).astype(jnp.bfloat16)
    ids = jnp.dot(agg[...].astype(f32).astype(jnp.bfloat16), expand, preferred_element_type=f32)
    for b in range(rows // H):
        C[3, H + b * H:2 * H + b * H, :] = jnp.broadcast_to(ids[b:b + 1, :], (H, LANES))

    def raw(ref, g, r, stride):
        return ref[pl.ds(g * H * stride + r, H, stride), :]

    local[0].wait()
    local[1].wait()

    def pack(r, _):
        east = west = None
        for q in reversed(range(4)):
            row = q * quarter + r
            m = [turn(raw(xr, g, row, rows), 16 * g) for g in range(ng)]
            for g in range(ng):
                XW[H + row, g * H:(g + 1) * H, :] = m[g]
            both = m[ng - 1]
            for g in range(ng - 1):
                both = jnp.where(win[g], m[g], both)
            fe = turn(both, H * (q % 2) + 48 * (q // 2))
            fw = turn(both, -H * (q % 2) + 48 * (q // 2))
            if q == 3:
                east, west = fe, fw
            else:
                low = (LL < 48) if q < 2 else (LL < 96)
                ea = in_a if q % 2 == 0 else ~in_a
                wa = ~in_a if q % 2 == 0 else in_a
                east = jnp.where(low & ea, fe, east)
                west = jnp.where(low & wa, fw, west)
        for q in range(4):
            for g in range(ng):
                to = 88 + 4 * g + q
                west = jnp.where(lane == to, turn(raw(pr, g, q * quarter + r, rows), to), west)
        toe[r] = east
        tow[r] = west
        return 0

    loop(quarter, pack, 0, 4)
    for g in range(ng):
        part[g * H:(g + 1) * H, :] = raw(pr, g, 0, rows)
    local[2].wait()
    local[3].wait()
    half = rows // 2
    lane_h = lax.broadcasted_iota(jnp.int32, (half, LANES), 1)
    LLh = lax.rem(lane_h + H, LANES)

    def coef_pack(lo):
        total = C[3, H + lo:H + lo + half, :]
        total = turn(total, 48)
        for n in range(3):
            total = jnp.where(LLh // 16 == n, turn(C[n, H + lo:H + lo + half, :], 16 * n), total)
        return total

    pc[...] = jnp.where(LLh < 64, coef_pack(0), turn(coef_pack(half), 64))
    def gram_loop(make_lhs, make_rhs):
        def body(n, total):
            lhs = jnp.concatenate([jnp.concatenate(make_lhs(2 * n + k), axis=0) for k in range(2)], axis=1)
            rhs = lhs if make_rhs is None else jnp.concatenate(
                [jnp.concatenate(make_rhs(2 * n + k), axis=0) for k in range(2)], axis=1)
            lh = jnp.concatenate(split2(lhs), axis=0)
            return total + dot_last(lh, lh if make_rhs is None else jnp.concatenate(split2(rhs), axis=0))
        return loop(rows // 2, body, jnp.zeros((4 * count, 4 * count), f32), 8)

    def trial_rows(r):
        return [raw(xr, g, r, rows) for g in range(ng)] + [raw(pr, g, r, rows) for g in range(ng)]

    early_b = gram_loop(trial_rows, None)
    pl.semaphore_wait(barrier, len(greeted))

    last = quarter - H
    moves = {
        (-1, 0): [(x3.at[:, 0:H], bot), (C.at[:, H:2 * H], C.at[:, H + rows:ext]), (part, pb)],
        (1, 0): [(x3.at[:, rows - H:rows], top), (C.at[:, rows:rows + H], C.at[:, 0:H])],
        (0, 1): [(toe, wb), (pc, wc)],
        (0, -1): [(tow, eb), (pc, ec)],
        (-1, 1): [(toe.at[0:H], swb), (pc.at[0:H], swc)],
        (-1, -1): [(tow.at[0:H], seb), (pc.at[0:H], sec)],
        (1, 1): [(toe.at[last:quarter], nwb), (pc.at[half - H:half], nwc)],
        (1, -1): [(tow.at[last:quarter], neb), (pc.at[half - H:half], nec)],
    }

    def exists(dx, dy):
        return (i + dx >= 0) & (i + dx < ngx) & (j + dy >= 0) & (j + dy < ngy)

    def copies_of(d):
        base = 3 * list(moves).index(d)
        return [remote(src, dst, hs.at[base + n], hr.at[base + n], (i + d[0], j + d[1]))
                for n, (src, dst) in enumerate(moves[d])]

    for d in moves:
        @pl.when(exists(*d))
        def _(d=d):
            for copy in copies_of(d):
                copy.start()

        @pl.when(jnp.logical_not(exists(-d[0], -d[1])))
        def _(d=d):
            for _, dst in moves[d]:
                dst[...] = jnp.zeros(dst.shape, dst.dtype)

    mine = lax.broadcasted_iota(jnp.int32, (1, LANES), 1)
    CI[i, z, c] = jnp.where(mine == 0, cols[0, 0], jnp.where(mine == 1, cols[0, 1], cols[0, 2]))
    local[4].wait()
    v1 = []
    for n, p in enumerate(peers_z):
        v1.append(remote(VA.at[i, z, c], VA.at[i, z, c], vs.at[2 * n], vr.at[2 * n], p))
        v1.append(remote(CI.at[i, z, c], CI.at[i, z, c], vs.at[2 * n + 1], vr.at[2 * n + 1], p))
    for copy in v1:
        copy.start()

    for ref in (S, B):
        for row in (0, 1, ext - 2, ext - 1):
            ref[row] = jnp.zeros(ref.shape[1:], f32)

    for d in moves:
        @pl.when(exists(-d[0], -d[1]))
        def _(d=d):
            for copy in copies_of(d):
                copy.wait_recv()

    for ref, at in ((top, 0), (bot, H + rows)):
        flat = ref.reshape(count * H, LANES)
        for r in range(H):
            for g in range(ng):
                XW[at + r, g * H:(g + 1) * H, :] = turn(raw(flat, g, r, H), 16 * g)

    def edge(w, e, q):
        w = turn(w, -(H * (q % 2) + 48 * (q // 2)))
        e = turn(e, H * (q % 2) - 48 * (q // 2))
        return jnp.where(in_win, jnp.where(in_a, w, e), 0.0)

    at_e = slice(ng * H, (ng + 1) * H)

    def unpack(r, _):
        for q in range(4):
            XW[H + q * quarter + r, at_e, :] = edge(wb[r], eb[r], q)
        return 0

    loop(quarter, unpack, 0, 8)
    for r in range(H):
        XW[r, at_e, :] = edge(nwb[r], neb[r], 3)
        XW[H + rows + r, at_e, :] = edge(swb[r], seb[r], 0)

    def masks(number):
        ln = lax.broadcasted_iota(jnp.int32, (number, LANES), 1)
        return ln, lax.rem(ln + H, LANES)

    def joined(w, e):
        _, l2 = masks(w.shape[0])
        return jnp.where(lax.rem(l2, 16) < 8, w, e)

    side = joined(wc[...], ec[...])
    wide = jnp.concatenate([turn(joined(nwc[...], nec[...]), 64), side, turn(side, 64),
                            joined(swc[...], sec[...])], axis=0)
    lnx, llx = masks(ext)

    def fields(n):
        m = C[n]
        res = [turn(m, 16 * g) for g in range(ng)]
        e = jnp.zeros_like(wide)
        for g in range(ng):
            e = jnp.where(llx // 16 == g, turn(wide, 16 * (g - n)), e)
        return res + [e]

    def lefts(v, ml):
        l = [turn(a, 1) for a in v]
        e = l[ng]
        for g in range(ng):
            e = jnp.where(ml[g], l[g], e)
        return [jnp.where(ml[g], l[ng], l[g]) for g in range(ng)] + [e]

    def rights(v, mr):
        l = [turn(a, LANES - 1) for a in v]
        e = l[ng]
        for g in range(ng):
            e = jnp.where(mr[g], l[g], e)
        return [jnp.where(mr[g], l[ng], l[g]) for g in range(ng)] + [e]

    cx, cy, sh, ag = fields(0), fields(1), fields(2), fields(3)
    mlx = [lnx == 16 * g for g in range(ng)]
    py = lefts(cy, mlx)
    for g in range(ng + 1):
        px = pltpu.roll(cx[g], 1, 0)
        diag = cx[g] + px + cy[g] + py[g] + sh[g]
        inside = sh[g] > 0.0
        inv = jnp.where(inside, 1.0 / jnp.where(inside, diag, 1.0), 0.0)
        CO[CXS, g] = inv * cx[g]
        CO[PXS, g] = inv * px
        CO[CYS, g] = inv * cy[g]
        CO[PYS, g] = inv * py[g]
        CO[DIA, g] = diag
        CO[INV, g] = inv
        CO[AGG, g] = ag[g]

    def coef(n, g, r):
        return jnp.broadcast_to(CO[n, g, pl.ds(r, 1), :], (H, LANES))

    every = range(ng + 1)
    main = range(ng)

    def get(ref, r, groups=every):
        return [ref[r, g * H:(g + 1) * H, :] for g in groups]

    def put(ref, r, v):
        for g, a in enumerate(v):
            ref[r, g * H:(g + 1) * H, :] = a

    def spreadout(r, vm, vc, vp):
        rt, lf = rights(vc, at_r), lefts(vc, at_l)
        return [coef(CXS, g, r) * vp[g] + coef(PXS, g, r) * vm[g]
                + coef(CYS, g, r) * rt[g] + coef(PYS, g, r) * lf[g] for g in every]

    def march(make, finish, first, number, unroll):
        def body(n, carry):
            vm, vc = carry
            for k in range(unroll):
                r = first + 1 + n * unroll + k
                vp = make(r + 1, k)
                finish(r, vc, spreadout(r, vm, vc, vp))
                vm, vc = vc, vp
            return vm, vc
        lax.fori_loop(0, number // unroll, body, (make(first, None), make(first + 1, None)))

    def fin_image(r, vc, t):
        put(B, r, [vc[g] - t[g] for g in every])

    march(lambda r, k: get(XW, r), fin_image, 1, ext - 4, 20)

    def ratio(n, carry):
        num, den = carry
        num, den = list(num), list(den)
        for k in range(4):
            r = H + n * 4 + k
            for g in main:
                xv = XW[r, g * H:(g + 1) * H, :]
                num[g] = num[g] + xv * (coef(DIA, g, r) * B[r, g * H:(g + 1) * H, :])
                den[g] = den[g] + xv * xv
        return tuple(num), tuple(den)

    zero = jnp.zeros((H, LANES), f32)
    num, den = loop(rows // 4, ratio, ((zero,) * ng, (zero,) * ng), 4)
    nd = zero
    for g in main:
        nd = jnp.where(lane == 2 * g, jnp.sum(num[g], axis=1, keepdims=True), nd)
        nd = jnp.where(lane == 2 * g + 1, jnp.sum(den[g], axis=1, keepdims=True), nd)

    def summed(slots, number):
        total = slots[0]
        for n in range(1, number):
            total = total + slots[n]
        return total

    def begin(copies):
        for copy in copies:
            copy.start()
        return copies

    def finish_all(copies):
        for copy in copies:
            copy.wait()

    n1[j] = nd
    c1 = begin([remote(n1.at[j], n1.at[j], ns1.at[n], nr1.at[n], p) for n, p in enumerate(peers_y)])

    def forward(r, _):
        for q in range(4):
            row = q * quarter + r
            for g in main:
                pv = raw(pr, g, row, rows)
                nxt = turn(eb[r], LANES - 1 - (88 + 4 * g + q))
                rt = jnp.where(lane == LANES - 1, nxt, turn(pv, LANES - 1))
                below = raw(pr, g, jnp.minimum(row + 1, rows - 1), rows)
                below = jnp.where(row == rows - 1, pb[g * H:(g + 1) * H, :], below)
                TP[row, g * H:(g + 1) * H, :] = coef(DIA, 0, H + row) * (
                    0.5 * pv - coef(CXS, 0, H + row) * below - coef(CYS, 0, H + row) * rt)
        return 0

    loop(quarter, forward, 0, 4)
    finish_all(c1)
    n2[i] = summed(n1, ngy)
    c1 = begin([remote(n2.at[i], n2.at[i], ns2.at[n], nr2.at[n], p) for n, p in enumerate(peers_x)])

    def image_rows(n, _):
        for k in range(4):
            r = n * 4 + k
            for g in main:
                AX[r, g * H:(g + 1) * H, :] = turn(
                    coef(DIA, g, H + r) * B[H + r, g * H:(g + 1) * H, :], -16 * g)
        return 0

    loop(rows // 4, image_rows, 0, 4)
    early_a = gram_loop(trial_rows, lambda r: [AX[r], TP[r]])
    finish_all(c1)
    nd = summed(n2, ngx)
    lam = []
    for g in main:
        a = jnp.sum(jnp.where(lane == 2 * g, nd, 0.0), axis=1, keepdims=True)
        b = jnp.sum(jnp.where(lane == 2 * g + 1, nd, 0.0), axis=1, keepdims=True)
        lam.append(jnp.broadcast_to(a / b, (H, LANES)))
    lam_e = lam[ng - 1]
    for g in range(ng - 1):
        lam_e = jnp.where(win[g], lam[g], lam_e)
    lam = lam + [lam_e]

    finish_all(v1)
    v2 = []
    for n, p in enumerate(peers_x):
        at = 2 * (nz - 1 + n)
        v2.append(remote(VA.at[i, :, c], VA.at[i, :, c], vs.at[at], vr.at[at], p))
        v2.append(remote(CI.at[i, :, c], CI.at[i, :, c], vs.at[at + 1], vr.at[at + 1], p))
    begin(v2)

    def make1(r, k):
        b, xv = get(B, r), get(XW, r)
        d = [(b[g] - lam[g] * (coef(INV, g, r) * xv[g])) * (1.0 / theta) for g in every]
        put(D1, r, d)
        return d

    def fin1(r, d, t):
        put(S, r, [(theta - 1.0) * d[g] + t[g] for g in every])

    def make2(r, k):
        d, s = get(D1, r), get(S, r)
        d = [CHEB[0][0] * d[g] + CHEB[0][1] * s[g] for g in every]
        put(D2, r, d)
        return d

    def fin_s(r, d, t):
        s = get(S, r)
        put(S, r, [s[g] - d[g] + t[g] for g in every])

    def make3(r, k):
        d1, d2, s = get(D1, r), get(D2, r), get(S, r)
        d = [CHEB[1][0] * d2[g] + CHEB[1][1] * s[g] for g in every]
        put(SM, r, [d1[g] + d2[g] + d[g] for g in every])
        return d

    march(make1, fin1, 1, ext - 4, 20)
    march(make2, fin_s, 1, ext - 4, 20)
    march(make3, fin_s, 1, ext - 4, 20)

    groups = near.shape[2]
    per = 2
    ids_t = lax.broadcasted_iota(jnp.int32, (groups, LANES), 0)

    def block_sum(b, _):
        for g in main:
            total = None
            for k in range(H):
                r = H + b * H + k
                term = coef(DIA, g, r) * S[r, g * H:(g + 1) * H, :]
                total = term if total is None else total + term
            RS[b, g * H:(g + 1) * H, :] = turn(total, -16 * g)
        return 0

    loop(rows // H, block_sum, 0, 4)

    def gathered(b, total):
        parts, hots = [], []
        for k in range(per):
            parts.append(RS[b * per + k])
            own = CO[AGG, 0, pl.ds(H + (b * per + k) * H, 1), :].astype(jnp.int32)
            hots.append(jnp.where(ids_t == own, 1.0, 0.0).astype(jnp.bfloat16))
        high, low = split2(jnp.concatenate(parts, axis=1))
        return total + dot_last(jnp.concatenate([high, low], axis=0), jnp.concatenate(hots, axis=1))

    total = loop(rows // H // per, gathered, jnp.zeros((2 * count, groups), f32), 8)
    rhs = total[:count] + total[count:]

    own_rhs = G0.at[me]
    own_rhs[...] = rhs
    cs = begin([remote(own_rhs, own_rhs, gs1.at[n], gr1.at[n], p) for n, p in enumerate(peers_y)])
    finish_all(v2)
    v3 = begin([remote(VA.at[:, :, c], VA.at[:, :, c], vs.at[2 * (nz + ngx - 2)], vr.at[2 * (nz + ngx - 2)], partner),
                remote(CI.at[:, :, c], CI.at[:, :, c], vs.at[2 * (nz + ngx - 2) + 1], vr.at[2 * (nz + ngx - 2) + 1], partner)])
    finish_all(cs)
    line = G0.at[pl.ds(i * ngy, ngy)]
    cs = begin([remote(line, line, gs2.at[n], gr2.at[n], p) for n, p in enumerate(peers_x)])
    finish_all(v3)
    listed = pltpu.make_async_copy(CI, SC, dloc.at[6])
    listed.start()
    listed.wait()
    finish_all(cs)
    ndev = ngx * ngy
    every_vals = VA.reshape(ndev, 3 * groups, groups)
    every_cols = SC.reshape(ndev, 1, LANES)
    eye = (lax.broadcasted_iota(jnp.int32, (groups, groups), 0)
           == lax.broadcasted_iota(jnp.int32, (groups, groups), 1))

    def scale(d):
        full = jnp.where(eye, every_vals[d, 0:groups, :].astype(f32), 0.0)
        return damping / jnp.sum(full, axis=0, keepdims=True)

    def columns(d):
        return [every_cols[d, 0, n] for n in (1, 2)]

    def update(d, own, others, factor):
        lhs = jnp.concatenate(split2(jnp.concatenate([own] + others, axis=1)), axis=0)
        weights = jnp.concatenate([every_vals[d, n * groups:(n + 1) * groups, :] for n in range(3)], axis=1)
        total = dot_last(lhs, weights)
        return own + factor * (G0[d] - total[:count] - total[count:])

    ring1 = [me] + columns(me)
    first = [(d, scale(d)) for d in ring1]
    second = {}
    for n in (1, 2):
        for k, d in enumerate(columns(ring1[n])):
            second[(n, k)] = (d, scale(d))
    z1 = [G0[d] * f for d, f in first]
    z2 = {key: G0[d] * f for key, (d, f) in second.items()}
    y2 = {}
    for key, (d, f) in second.items():
        y2[key] = update(d, z2[key], [G0[q] * scale(q) for q in columns(d)], f)
    y1 = [update(d, z1[n], z1[1:] if n == 0 else [z2[(n, 0)], z2[(n, 1)]], f) for n, (d, f) in enumerate(first)]
    x1 = [update(d, y1[n], y1[1:] if n == 0 else [y2[(n, 0)], y2[(n, 1)]], f) for n, (d, f) in enumerate(first)]
    e = update(me, x1[0], x1[1:], first[0][1])
    tiles = 2 * count // H

    near[4] = e
    cs = begin([remote(near.at[4], near.at[3 * s + t], as_.at[n], ar_.at[n], wrapped(1 - s, 1 - t))
                for n, (s, t) in enumerate(steps)])
    finish_all(cs)

    def spread(b, _):
        s = jnp.where(b == 0, 0, jnp.where(b == ext // H - 1, 2, 1))
        res = []
        for g in main:
            idx = coef(AGG, g, b * H).astype(jnp.int32)
            own = jnp.take_along_axis(near[3 * s + 1, g * H:(g + 1) * H, :], idx, axis=1)
            res.append(jnp.where(coef(INV, g, b * H) > 0.0, own, 0.0))
        idx = coef(AGG, ng, b * H).astype(jnp.int32)
        ev = jnp.zeros((H, LANES), f32)
        for g in main:
            lf = jnp.take_along_axis(near[3 * s, g * H:(g + 1) * H, :], idx, axis=1)
            rt = jnp.take_along_axis(near[3 * s + 2, g * H:(g + 1) * H, :], idx, axis=1)
            ev = jnp.where(win[g], jnp.where(in_a, lf, rt), ev)
        res.append(jnp.where(coef(INV, ng, b * H) > 0.0, ev, 0.0))
        put(FA, b, res)
        put(FR, b, rights(res, at_r))
        put(FL, b, lefts(res, at_l))
        return 0

    loop(ext // H, spread, 0, 6)

    def make4(r, k):
        b = r // H
        f, fr, fl = get(FA, b), get(FR, b), get(FL, b)
        up = f if k is None or k % 4 != 3 else get(FA, (r + 1) // H)
        dn = f if k is None or k % 4 != 0 else get(FA, (r - 1) // H)
        s, x = get(S, r), get(SM, r)
        d, nx = [], []
        for g in every:
            v = s[g] - f[g] + (coef(CXS, g, r) * up[g] + coef(PXS, g, r) * dn[g]
                               + coef(CYS, g, r) * fr[g] + coef(PYS, g, r) * fl[g])
            v = v * (1.0 / theta)
            d.append(v)
            nx.append(x[g] + f[g] + v)
        put(D1, r, d)
        put(SM, r, nx)
        return d

    def make5(r, k):
        d, s, x = get(D1, r), get(S, r), get(SM, r)
        d = [CHEB[0][0] * d[g] + CHEB[0][1] * s[g] for g in every]
        put(D2, r, d)
        put(SM, r, [x[g] + d[g] for g in every])
        return d

    def make6(r, k):
        d, s, x = get(D2, r), get(S, r), get(SM, r)
        return [x[g] + (CHEB[1][0] * d[g] + CHEB[1][1] * s[g]) for g in every]

    W, AW = D1, B

    def fin6(r, w, t):
        for g in main:
            v = turn(w[g], -16 * g)
            W[r, g * H:(g + 1) * H, :] = v
            xw_out[pl.ds(g * H * rows + r - H, H, rows), :] = v
            AW[r, g * H:(g + 1) * H, :] = turn(coef(DIA, g, r) * (w[g] - t[g]), -16 * g)

    march(make4, fin1, 2, ext - 4, 20)
    march(make5, fin_s, 5, rows + 4, 22)

    march(make6, fin6, 7, rows, 16)
    store = pltpu.make_async_copy(xw_out, out, dloc.at[5])
    store.start()

    def gram_late(n, total):
        halves = []
        for k in range(2):
            r = 2 * n + k
            halves.append(jnp.concatenate(
                [raw(xr, g, r, rows) for g in main]
                + [W[H + r, 0:count, :]] + [raw(pr, g, r, rows) for g in main]
                + [W[H + r, 0:count, :], AW[H + r, 0:count, :]], axis=0))
        both = jnp.concatenate(halves, axis=1)
        high, low = split2(both)
        lhs = jnp.concatenate([high[3 * count:], low[3 * count:]], axis=0)
        rhs_ = jnp.concatenate([high[:3 * count], low[:3 * count]], axis=0)
        return total + dot_last(lhs, rhs_)

    late = loop(rows // 2, gram_late, jnp.zeros((4 * count, 6 * count), f32), 8)

    def folded(total, width):
        total = total[:2 * count] + total[2 * count:]
        total = total[:, :width] + total[:, width:]
        return jnp.concatenate([total, jnp.zeros((2 * count, LANES - width), f32)], axis=1)

    early = jnp.concatenate([folded(early_b, 2 * count)[:, :2 * count], folded(early_a, 2 * count)[:, :LANES - 2 * count]],
                            axis=1)
    late = folded(late, 3 * count)
    for t in range(tiles):
        t1[t, 0] = early[t * H:(t + 1) * H]
        t1[t, 1] = late[t * H:(t + 1) * H]

    def each_owner(act):
        for t in range(tiles):
            @pl.when(j != t)
            def _(t=t):
                act(t)

    each_owner(lambda t: remote(t1.at[t], u1.at[j], es1.at[t], er1.at[j], (i, t)).start())

    @pl.when(j < tiles)
    def _():
        u1[j] = t1[j]
        for o in range(1, ngy):
            src = lax.rem(j + o, ngy)
            remote(t1.at[0], u1.at[src], es1.at[0], er1.at[src], (i, src)).wait_recv()
        u2[i] = summed(u1, ngy)
        cx_ = begin([remote(u2.at[i], u2.at[i], es2.at[n], er2.at[n], p) for n, p in enumerate(peers_x)])
        finish_all(cx_)
        u3[j] = summed(u2, ngx)
        for o in range(1, ngy):
            remote(u3.at[j], u3.at[j], es3.at[o], er3.at[j], (i, lax.rem(j + o, ngy))).start()
        for o in range(1, ngy):
            remote(u3.at[j], u3.at[j], es3.at[o], er3.at[j], (i, lax.rem(j + o, ngy))).wait_send()

    each_owner(lambda t: remote(t1.at[t], u1.at[j], es1.at[t], er1.at[j], (i, t)).wait_send())
    each_owner(lambda t: remote(u3.at[t], u3.at[t], es3.at[0], er3.at[t], (i, t)).wait_recv())

    E = jnp.concatenate([u3[t, 0] for t in range(tiles)], axis=0)
    L = jnp.concatenate([u3[t, 1] for t in range(tiles)], axis=0)
    k = count
    pad = jnp.zeros((LANES - 2 * k, LANES), f32)
    ET = jnp.concatenate([E, pad], axis=0).T
    LT = jnp.concatenate([L, pad], axis=0).T

    def cat(blocks):
        return jnp.concatenate([jnp.concatenate(line, axis=1) for line in blocks], axis=0)

    gb_ref[...] = cat([[E[0:k, 0:k], LT[0:k, 0:k], E[0:k, k:2 * k]],
                       [L[0:k, 0:k], L[0:k, k:2 * k], L[0:k, 2 * k:3 * k]],
                       [E[k:2 * k, 0:k], LT[2 * k:3 * k, 0:k], E[k:2 * k, k:2 * k]]])
    ga_ref[...] = cat([[E[0:k, 2 * k:3 * k], LT[0:k, k:2 * k], ET[2 * k:3 * k, k:2 * k]],
                       [L[k:2 * k, 0:k], L[k:2 * k, k:2 * k], L[k:2 * k, 2 * k:3 * k]],
                       [E[k:2 * k, 2 * k:3 * k], LT[2 * k:3 * k, k:2 * k],
                        E[k:2 * k, 3 * k:4 * k] + ET[3 * k:4 * k, k:2 * k]]])
    store.wait()
    for d in moves:
        @pl.when(exists(*d))
        def _(d=d):
            for copy in copies_of(d):
                copy.wait_send()


def per_device(eigvecs, search_dir, conduct, shift, aggregate, coarse_cols, coarse_vals):
    count, rows, width = eigvecs.shape
    groups = coarse_vals.shape[2]
    ngx, ngy = lax.axis_size("gx"), lax.axis_size("gy")
    ext = rows + 2 * H
    ng = count // H
    quarter, half = rows // 4, rows // 2
    lines = (ng + 1) * H
    tiles = 2 * count // H
    dma = pltpu.SemaphoreType.DMA
    v = pltpu.VMEM

    def fl(*shape):
        return v(shape, f32)

    scratch = [
        fl(count * rows, width), fl(count * rows, width), fl(4, ext, width),
        fl(count, H, width), fl(count, H, width), fl(count, width),
        fl(quarter, H, LANES), fl(quarter, H, LANES), fl(half, LANES),
        fl(quarter, H, LANES), fl(quarter, H, LANES), fl(half, LANES), fl(half, LANES),
        fl(H, H, LANES), fl(H, H, LANES), fl(H, H, LANES), fl(H, H, LANES),
        fl(H, LANES), fl(H, LANES), fl(H, LANES), fl(H, LANES),
        fl(ext, lines, LANES), fl(ext, lines, LANES), fl(ext, lines, LANES), fl(ext, lines, LANES),
        fl(ext, lines, LANES), fl(ext, lines, LANES),
        fl(rows, count, LANES), fl(rows, count, LANES),
        fl(7, ng + 1, ext, LANES),
        fl(ngy, H, LANES), fl(ngx, H, LANES),
        v((ngx, ngy // 2, 2, 3 * groups, groups), jnp.bfloat16),
        v((ngx, ngy // 2, 2, 1, LANES), jnp.int32), pltpu.SMEM((ngx, ngy // 2, 2, 1, LANES), jnp.int32),
        fl(ngx * ngy, count, groups),
        fl(rows // H, count, LANES),
        fl(9, count, groups),
        fl(ext // H + 1, lines, LANES), fl(ext // H, lines, LANES), fl(ext // H, lines, LANES),
        fl(count * rows, width), fl(tiles, 2, H, LANES),
        fl(ngy, 2, H, LANES), fl(ngx, 2, H, LANES), fl(ngy, 2, H, LANES),
        fl(count, LANES),
        dma((7,)), dma((24,)), dma((24,)),
        dma((ngy - 1,)), dma((ngy - 1,)), dma((ngx - 1,)), dma((ngx - 1,)),
        dma((ngy - 1,)), dma((ngy - 1,)), dma((ngx - 1,)), dma((ngx - 1,)),
        dma((8,)), dma((8,)),
        dma((tiles,)), dma((ngy,)), dma((ngx - 1,)), dma((ngx - 1,)), dma((ngy,)), dma((ngy,)),
        dma((ngy + 2 * ngx,)), dma((ngy + 2 * ngx,)),
    ]
    anyspace = pl.BlockSpec(memory_space=pl.ANY)
    vmem = pl.BlockSpec(memory_space=pltpu.VMEM)
    smem = pl.BlockSpec(memory_space=pltpu.SMEM)
    size = 3 * count
    out, ga, gb = pl.pallas_call(
        functools.partial(kernel, ngx, ngy, rows),
        out_shape=[jax.ShapeDtypeStruct((count * rows, width), f32),
                   jax.ShapeDtypeStruct((size, size), f32), jax.ShapeDtypeStruct((size, size), f32)],
        in_specs=[anyspace, anyspace, anyspace, anyspace, anyspace, vmem, smem, anyspace],
        out_specs=[anyspace, vmem, vmem],
        scratch_shapes=scratch,
        compiler_params=pltpu.CompilerParams(vmem_limit_bytes=VMEM_CAP, collective_id=0, has_side_effects=True),
        name="step",
    )(eigvecs.reshape(count * rows, width), eigvecs, search_dir.reshape(count * rows, width), conduct, shift,
      aggregate, coarse_cols, coarse_vals.reshape(-1, groups))
    return out.reshape(count, rows, width), ga, gb


def solution(mesh):
    placed = (
        P(None, "gx", "gy"),
        P(None, "gx", "gy"),
        P(None, "gx", "gy"),
        P("gx", "gy"),
        P("gx", "gy"),
        P(("gx", "gy"), None),
        P(("gx", "gy"), None, None, None),
    )
    return jax.shard_map(
        per_device,
        mesh=mesh,
        in_specs=placed,
        out_specs=(P(None, "gx", "gy"), P(), P()),
        check_vma=False,
    )
```

```python
import functools

import jax
import jax.numpy as jnp
from jax import lax
from jax.experimental import pallas as pl
from jax.experimental.pallas import tpu as pltpu
from jax.sharding import PartitionSpec as P

H = 8
LANES = 128
VMEM_CAP = 60 * 1024 * 1024

cheb_lo = 0.3
cheb_hi = 2.0
damping = 0.6
theta = (cheb_hi + cheb_lo) / 2.0
delta = (cheb_hi - cheb_lo) / 2.0
sigma = theta / delta
RHO0 = 1.0 / sigma
RHO1 = 1.0 / (2.0 * sigma - RHO0)
RHO2 = 1.0 / (2.0 * sigma - RHO1)
CHEB = ((RHO1 * RHO0, 2.0 * RHO1 / delta), (RHO2 * RHO1, 2.0 * RHO2 / delta))

CONTRACT_LAST = (((1,), (1,)), ((), ()))
CXS, PXS, CYS, PYS, DIA, INV, AGG = range(7)
f32 = jnp.float32


def loop(number, body, carry, unroll):
    def several(n, carry):
        for k in range(unroll):
            carry = body(n * unroll + k, carry)
        return carry
    return lax.fori_loop(0, number // unroll, several, carry)


def split2(value):
    high = value.astype(jnp.bfloat16)
    low = (value - high.astype(f32)).astype(jnp.bfloat16)
    return high, low


def turn(value, by):
    by = by % LANES
    return pltpu.roll(value, by, 1) if by else value


def dot_last(a, b):
    return lax.dot_general(a, b, CONTRACT_LAST, preferred_element_type=f32)


def remote(src, dst, send, recv, peer):
    return pltpu.make_async_remote_copy(src_ref=src, dst_ref=dst, send_sem=send, recv_sem=recv,
                                        device_id=peer, device_id_type=pl.DeviceIdType.MESH)


def kernel(ngx, ngy, rows, x2, x3, p2, cond, shift, agg, cols, vals, out, ga_ref, gb_ref,
           xr, pr, C, top, bot, pb, toe, tow, pc, wb, eb, wc, ec, nwb, neb, swb, seb, nwc, nec, swc, sec,
           XW, B, S, D1, D2, SM, AX, TP, CO, n1, n2, VA, CI, SC, G0, RS, near, FA, FR, FL,
           xw_out, t1, u1, u2, u3, part, dloc, hs, hr, ns1, nr1, ns2, nr2, gs1, gr1, gs2, gr2, as_, ar_,
           es1, er1, es2, er2, es3, er3, vs, vr, ws, wr, tpw, tpe, ps):
    count = x3.shape[0]
    ext = rows + 2 * H
    ng = count // H
    quarter = rows // 4
    i, j = lax.axis_index("gx"), lax.axis_index("gy")
    me = i * ngy + j
    nz = ngy // 2
    z, c = j // 2, lax.rem(j, 2)
    partner = (i, j + 1 - 2 * c)
    peers_z = [(i, lax.rem(z + o, nz) * 2 + c) for o in range(1, nz)]
    peers_y = [(i, lax.rem(j + o, ngy)) for o in range(1, ngy)]
    peers_x = [(lax.rem(i + o, ngx), j) for o in range(1, ngx)]
    peers_xc = [(ii, j) for ii, _ in peers_x] + [partner] + [(ii, partner[1]) for ii, _ in peers_x]
    steps = [(s, t) for s in range(3) for t in range(3) if (s, t) != (1, 1)]

    def wrapped(dx, dy):
        return (lax.rem(i + dx + ngx, ngx), lax.rem(j + dy + ngy, ngy))

    lane = lax.broadcasted_iota(jnp.int32, (H, LANES), 1)
    LL = lax.rem(lane + H, LANES)
    in_a = lax.rem(LL, 16) < 8
    win = [LL // 16 == g for g in range(ng)]
    in_win = LL < 16 * ng
    at_r = [lane == (16 * g - 1) % LANES for g in range(ng)]
    at_l = [lane == 16 * g for g in range(ng)]

    def begin(copies):
        for copy in copies:
            copy.start()
        return copies

    def finish_all(copies):
        for copy in copies:
            copy.wait()

    local = [pltpu.make_async_copy(x2, xr, dloc.at[0]), pltpu.make_async_copy(p2, pr, dloc.at[1]),
             pltpu.make_async_copy(cond, C.at[0:2, H:H + rows], dloc.at[2]),
             pltpu.make_async_copy(shift, C.at[2, H:H + rows], dloc.at[3]),
             pltpu.make_async_copy(vals, VA.at[i, z, c], dloc.at[4])]
    for copy in local:
        copy.start()

    diagonal = [wrapped(dx, dy) for dx in (-1, 1) for dy in (-1, 1)]
    greeted = peers_y + peers_x + diagonal + [(ii, partner[1]) for ii, _ in peers_x]
    barrier = pltpu.get_barrier_semaphore()
    for peer in greeted:
        pl.semaphore_signal(barrier, inc=1, device_id=peer, device_id_type=pl.DeviceIdType.MESH)

    expand = jnp.where(lax.broadcasted_iota(jnp.int32, (agg.shape[1], LANES), 1) // H
                       == lax.broadcasted_iota(jnp.int32, (agg.shape[1], LANES), 0), 1.0, 0.0).astype(jnp.bfloat16)
    ids = jnp.dot(agg[...].astype(f32).astype(jnp.bfloat16), expand, preferred_element_type=f32)
    for b in range(rows // H):
        C[3, H + b * H:2 * H + b * H, :] = jnp.broadcast_to(ids[b:b + 1, :], (H, LANES))

    def raw(ref, g, r, stride):
        return ref[pl.ds(g * H * stride + r, H, stride), :]

    local[0].wait()
    local[1].wait()

    def pack(r, _):
        east = west = None
        for q in reversed(range(4)):
            row = q * quarter + r
            m = [turn(raw(xr, g, row, rows), 16 * g) for g in range(ng)]
            for g in range(ng):
                XW[H + row, g * H:(g + 1) * H, :] = m[g]
            both = m[ng - 1]
            for g in range(ng - 1):
                both = jnp.where(win[g], m[g], both)
            fe = turn(both, H * (q % 2) + 48 * (q // 2))
            fw = turn(both, -H * (q % 2) + 48 * (q // 2))
            if q == 3:
                east, west = fe, fw
            else:
                low = (LL < 48) if q < 2 else (LL < 96)
                ea = in_a if q % 2 == 0 else ~in_a
                wa = ~in_a if q % 2 == 0 else in_a
                east = jnp.where(low & ea, fe, east)
                west = jnp.where(low & wa, fw, west)
        toe[r] = east
        tow[r] = west
        return 0

    loop(quarter, pack, 0, 4)
    for g in range(ng):
        part[g * H:(g + 1) * H, :] = raw(pr, g, 0, rows)
    local[2].wait()
    local[3].wait()
    half = rows // 2
    lane_h = lax.broadcasted_iota(jnp.int32, (half, LANES), 1)
    LLh = lax.rem(lane_h + H, LANES)

    def coef_pack(lo):
        total = C[3, H + lo:H + lo + half, :]
        total = turn(total, 48)
        for n in range(3):
            total = jnp.where(LLh // 16 == n, turn(C[n, H + lo:H + lo + half, :], 16 * n), total)
        return total

    pc[...] = jnp.where(LLh < 64, coef_pack(0), turn(coef_pack(half), 64))
    def gram_loop(make_lhs, make_rhs):
        def body(n, total):
            lhs = jnp.concatenate([jnp.concatenate(make_lhs(2 * n + k), axis=0) for k in range(2)], axis=1)
            rhs = lhs if make_rhs is None else jnp.concatenate(
                [jnp.concatenate(make_rhs(2 * n + k), axis=0) for k in range(2)], axis=1)
            lh = jnp.concatenate(split2(lhs), axis=0)
            return total + dot_last(lh, lh if make_rhs is None else jnp.concatenate(split2(rhs), axis=0))
        return loop(rows // 2, body, jnp.zeros((4 * count, 4 * count), f32), 8)

    def trial_rows(r):
        return [raw(xr, g, r, rows) for g in range(ng)] + [raw(pr, g, r, rows) for g in range(ng)]

    pl.semaphore_wait(barrier, len(greeted))

    last = quarter - H
    moves = {
        (-1, 0): [(x3.at[:, 0:H], bot), (C.at[:, H:2 * H], C.at[:, H + rows:ext]), (part, pb)],
        (1, 0): [(x3.at[:, rows - H:rows], top), (C.at[:, rows:rows + H], C.at[:, 0:H])],
        (0, 1): [(toe, wb), (pc, wc)],
        (0, -1): [(tow, eb), (pc, ec)],
        (-1, 1): [(toe.at[0:H], swb), (pc.at[0:H], swc)],
        (-1, -1): [(tow.at[0:H], seb), (pc.at[0:H], sec)],
        (1, 1): [(toe.at[last:quarter], nwb), (pc.at[half - H:half], nwc)],
        (1, -1): [(tow.at[last:quarter], neb), (pc.at[half - H:half], nec)],
    }

    def exists(dx, dy):
        return (i + dx >= 0) & (i + dx < ngx) & (j + dy >= 0) & (j + dy < ngy)

    def copies_of(d):
        base = 3 * list(moves).index(d)
        return [remote(src, dst, hs.at[base + n], hr.at[base + n], (i + d[0], j + d[1]))
                for n, (src, dst) in enumerate(moves[d])]

    for d in moves:
        @pl.when(exists(*d))
        def _(d=d):
            for copy in copies_of(d):
                copy.start()

        @pl.when(jnp.logical_not(exists(-d[0], -d[1])))
        def _(d=d):
            for _, dst in moves[d]:
                dst[...] = jnp.zeros(dst.shape, dst.dtype)

    mine = lax.broadcasted_iota(jnp.int32, (1, LANES), 1)
    CI[i, z, c] = jnp.where(mine == 0, cols[0, 0], jnp.where(mine == 1, cols[0, 1], cols[0, 2]))
    local[4].wait()
    v1 = []
    for n, p in enumerate(peers_z):
        v1.append(remote(VA.at[i, z, c], VA.at[i, z, c], vs.at[2 * n], vr.at[2 * n], p))
        v1.append(remote(CI.at[i, z, c], CI.at[i, z, c], vs.at[2 * n + 1], vr.at[2 * n + 1], p))
    begin(v1)
    v2 = [[remote(VA.at[i, z, c], VA.at[i, z, c], vs.at[2 * (nz - 1 + n)], vr.at[2 * (nz - 1 + n)], p),
           remote(CI.at[i, z, c], CI.at[i, z, c], vs.at[2 * (nz - 1 + n) + 1], vr.at[2 * (nz - 1 + n) + 1], p)]
          for n, p in enumerate(peers_x)]
    for pair in v2:
        begin(pair)

    for ref in (S, B):
        for row in (0, 1, ext - 2, ext - 1):
            ref[row] = jnp.zeros(ref.shape[1:], f32)

    def pack_p(r, _):
        west = jnp.zeros((H, LANES), f32)
        for q in range(H):
            for g in range(ng):
                to = ng * q + g
                west = jnp.where(lane == to, turn(raw(pr, g, q * (rows // H) + r, rows), to), west)
        tpw[r] = west
        return 0

    loop(rows // H, pack_p, 0, 2)

    def side_p():
        return remote(tpw, tpe, ps.at[0], ps.at[1], (i, j - 1))

    @pl.when(exists(0, -1))
    def _():
        side_p().start()

    @pl.when(jnp.logical_not(exists(0, 1)))
    def _():
        tpe[...] = jnp.zeros(tpe.shape, f32)

    early_b = gram_loop(trial_rows, None)
    for d in moves:
        @pl.when(exists(-d[0], -d[1]))
        def _(d=d):
            for copy in copies_of(d):
                copy.wait_recv()

    for ref, at in ((top, 0), (bot, H + rows)):
        flat = ref.reshape(count * H, LANES)
        for r in range(H):
            for g in range(ng):
                XW[at + r, g * H:(g + 1) * H, :] = turn(raw(flat, g, r, H), 16 * g)

    def edge(w, e, q):
        w = turn(w, -(H * (q % 2) + 48 * (q // 2)))
        e = turn(e, H * (q % 2) - 48 * (q // 2))
        return jnp.where(in_win, jnp.where(in_a, w, e), 0.0)

    at_e = slice(ng * H, (ng + 1) * H)

    def unpack(r, _):
        for q in range(4):
            XW[H + q * quarter + r, at_e, :] = edge(wb[r], eb[r], q)
        return 0

    loop(quarter, unpack, 0, 8)
    for r in range(H):
        XW[r, at_e, :] = edge(nwb[r], neb[r], 3)
        XW[H + rows + r, at_e, :] = edge(swb[r], seb[r], 0)

    def masks(number):
        ln = lax.broadcasted_iota(jnp.int32, (number, LANES), 1)
        return ln, lax.rem(ln + H, LANES)

    def joined(w, e):
        _, l2 = masks(w.shape[0])
        return jnp.where(lax.rem(l2, 16) < 8, w, e)

    side = joined(wc[...], ec[...])
    wide = jnp.concatenate([turn(joined(nwc[...], nec[...]), 64), side, turn(side, 64),
                            joined(swc[...], sec[...])], axis=0)
    lnx, llx = masks(ext)

    def fields(n):
        m = C[n]
        res = [turn(m, 16 * g) for g in range(ng)]
        e = jnp.zeros_like(wide)
        for g in range(ng):
            e = jnp.where(llx // 16 == g, turn(wide, 16 * (g - n)), e)
        return res + [e]

    def lefts(v, ml):
        l = [turn(a, 1) for a in v]
        e = l[ng]
        for g in range(ng):
            e = jnp.where(ml[g], l[g], e)
        return [jnp.where(ml[g], l[ng], l[g]) for g in range(ng)] + [e]

    def rights(v, mr):
        l = [turn(a, LANES - 1) for a in v]
        e = l[ng]
        for g in range(ng):
            e = jnp.where(mr[g], l[g], e)
        return [jnp.where(mr[g], l[ng], l[g]) for g in range(ng)] + [e]

    cx, cy, sh, ag = fields(0), fields(1), fields(2), fields(3)
    mlx = [lnx == 16 * g for g in range(ng)]
    py = lefts(cy, mlx)
    for g in range(ng + 1):
        px = pltpu.roll(cx[g], 1, 0)
        diag = cx[g] + px + cy[g] + py[g] + sh[g]
        inside = sh[g] > 0.0
        inv = jnp.where(inside, 1.0 / jnp.where(inside, diag, 1.0), 0.0)
        CO[CXS, g] = inv * cx[g]
        CO[PXS, g] = inv * px
        CO[CYS, g] = inv * cy[g]
        CO[PYS, g] = inv * py[g]
        CO[DIA, g] = diag
        CO[INV, g] = inv
        CO[AGG, g] = ag[g]

    def coef(n, g, r):
        return jnp.broadcast_to(CO[n, g, pl.ds(r, 1), :], (H, LANES))

    every = range(ng + 1)
    main = range(ng)

    def get(ref, r, groups=every):
        return [ref[r, g * H:(g + 1) * H, :] for g in groups]

    def put(ref, r, v):
        for g, a in enumerate(v):
            ref[r, g * H:(g + 1) * H, :] = a

    def spreadout(r, vm, vc, vp):
        rt, lf = rights(vc, at_r), lefts(vc, at_l)
        return [coef(CXS, g, r) * vp[g] + coef(PXS, g, r) * vm[g]
                + coef(CYS, g, r) * rt[g] + coef(PYS, g, r) * lf[g] for g in every]

    def march(make, finish, first, number, unroll):
        def body(n, carry):
            vm, vc = carry
            for k in range(unroll):
                r = first + 1 + n * unroll + k
                vp = make(r + 1, k)
                finish(r, vc, spreadout(r, vm, vc, vp))
                vm, vc = vc, vp
            return vm, vc
        lax.fori_loop(0, number // unroll, body, (make(first, None), make(first + 1, None)))

    def fin_image(r, vc, t):
        put(B, r, [vc[g] - t[g] for g in every])

    march(lambda r, k: get(XW, r), fin_image, 1, ext - 4, 20)

    def ratio(n, carry):
        num, den = carry
        num, den = list(num), list(den)
        for k in range(4):
            r = H + n * 4 + k
            for g in main:
                xv = XW[r, g * H:(g + 1) * H, :]
                num[g] = num[g] + xv * (coef(DIA, g, r) * B[r, g * H:(g + 1) * H, :])
                den[g] = den[g] + xv * xv
        return tuple(num), tuple(den)

    zero = jnp.zeros((H, LANES), f32)
    num, den = loop(rows // 4, ratio, ((zero,) * ng, (zero,) * ng), 4)
    nd = zero
    for g in main:
        nd = jnp.where(lane == 2 * g, jnp.sum(num[g], axis=1, keepdims=True), nd)
        nd = jnp.where(lane == 2 * g + 1, jnp.sum(den[g], axis=1, keepdims=True), nd)

    def summed(slots, number):
        total = slots[0]
        for n in range(1, number):
            total = total + slots[n]
        return total

    n1[j] = nd
    c1 = begin([remote(n1.at[j], n1.at[j], ns1.at[n], nr1.at[n], p) for n, p in enumerate(peers_y)])

    def forward(r, _):
        for q in range(H):
            row = q * (rows // H) + r
            for g in main:
                pv = raw(pr, g, row, rows)
                nxt = turn(tpe[r], LANES - 1 - (ng * q + g))
                rt = jnp.where(lane == LANES - 1, nxt, turn(pv, LANES - 1))
                below = raw(pr, g, jnp.minimum(row + 1, rows - 1), rows)
                below = jnp.where(row == rows - 1, pb[g * H:(g + 1) * H, :], below)
                TP[row, g * H:(g + 1) * H, :] = coef(DIA, 0, H + row) * (
                    0.5 * pv - coef(CXS, 0, H + row) * below - coef(CYS, 0, H + row) * rt)
        return 0

    finish_all(c1)
    n2[i] = summed(n1, ngy)
    c1 = begin([remote(n2.at[i], n2.at[i], ns2.at[n], nr2.at[n], p) for n, p in enumerate(peers_x)])

    finish_all(v1)
    for o in range(1, nz):
        zo = lax.rem(z + o, nz)
        for n, p in enumerate(peers_x):
            at = 2 * (nz - 1 + o * (ngx - 1) + n)
            v2[n] += begin([remote(VA.at[i, zo, c], VA.at[i, zo, c], vs.at[at], vr.at[at], p),
                            remote(CI.at[i, zo, c], CI.at[i, zo, c], vs.at[at + 1], vr.at[at + 1], p)])
    v3 = begin([remote(VA.at[i, :, c], VA.at[i, :, c], ws.at[0], wr.at[0], partner),
                remote(CI.at[i, :, c], CI.at[i, :, c], ws.at[1], wr.at[1], partner)])

    def image_rows(n, _):
        for k in range(4):
            r = n * 4 + k
            for g in main:
                AX[r, g * H:(g + 1) * H, :] = turn(
                    coef(DIA, g, H + r) * B[H + r, g * H:(g + 1) * H, :], -16 * g)
        return 0

    finish_all(c1)
    nd = summed(n2, ngx)
    lam = []
    for g in main:
        a = jnp.sum(jnp.where(lane == 2 * g, nd, 0.0), axis=1, keepdims=True)
        b = jnp.sum(jnp.where(lane == 2 * g + 1, nd, 0.0), axis=1, keepdims=True)
        lam.append(jnp.broadcast_to(a / b, (H, LANES)))
    lam_e = lam[ng - 1]
    for g in range(ng - 1):
        lam_e = jnp.where(win[g], lam[g], lam_e)
    lam = lam + [lam_e]

    def make1(r, k):
        b, xv = get(B, r), get(XW, r)
        d = [(b[g] - lam[g] * (coef(INV, g, r) * xv[g])) * (1.0 / theta) for g in every]
        put(D1, r, d)
        return d

    def fin1(r, d, t):
        put(S, r, [(theta - 1.0) * d[g] + t[g] for g in every])

    def make2(r, k):
        d, s = get(D1, r), get(S, r)
        d = [CHEB[0][0] * d[g] + CHEB[0][1] * s[g] for g in every]
        put(D2, r, d)
        return d

    def fin_s(r, d, t):
        s = get(S, r)
        put(S, r, [s[g] - d[g] + t[g] for g in every])

    def make3(r, k):
        d1, d2, s = get(D1, r), get(D2, r), get(S, r)
        d = [CHEB[1][0] * d2[g] + CHEB[1][1] * s[g] for g in every]
        put(SM, r, [d1[g] + d2[g] + d[g] for g in every])
        return d

    march(make1, fin1, 1, ext - 4, 20)
    march(make2, fin_s, 1, ext - 4, 20)
    march(make3, fin_s, 1, ext - 4, 20)

    groups = near.shape[2]
    per = 2
    ids_t = lax.broadcasted_iota(jnp.int32, (groups, LANES), 0)

    def block_sum(b, _):
        for g in main:
            total = None
            for k in range(H):
                r = H + b * H + k
                term = coef(DIA, g, r) * S[r, g * H:(g + 1) * H, :]
                total = term if total is None else total + term
            RS[b, g * H:(g + 1) * H, :] = turn(total, -16 * g)
        return 0

    loop(rows // H, block_sum, 0, 4)

    def gathered(b, total):
        parts, hots = [], []
        for k in range(per):
            parts.append(RS[b * per + k])
            own = CO[AGG, 0, pl.ds(H + (b * per + k) * H, 1), :].astype(jnp.int32)
            hots.append(jnp.where(ids_t == own, 1.0, 0.0).astype(jnp.bfloat16))
        high, low = split2(jnp.concatenate(parts, axis=1))
        return total + dot_last(jnp.concatenate([high, low], axis=0), jnp.concatenate(hots, axis=1))

    total = loop(rows // H // per, gathered, jnp.zeros((2 * count, groups), f32), 8)
    rhs = total[:count] + total[count:]

    own_rhs = G0.at[i, z, c]
    own_rhs[...] = rhs
    cs = begin([remote(own_rhs, own_rhs, gs1.at[n], gr1.at[n], p) for n, p in enumerate(peers_z)])
    loop(rows // 4, image_rows, 0, 4)
    @pl.when(exists(0, 1))
    def _():
        side_p().wait_recv()
    loop(rows // 8, forward, 0, 2)
    for n in range(ngx - 1):
        finish_all(v2[n])
        at = lax.rem(i + ngx - 1 - n, ngx)
        v3 += begin([remote(VA.at[at, :, c], VA.at[at, :, c], ws.at[2 * n + 2], wr.at[2 * n + 2], partner),
                     remote(CI.at[at, :, c], CI.at[at, :, c], ws.at[2 * n + 3], wr.at[2 * n + 3], partner)])
    finish_all(cs)
    line = G0.at[i, :, c]
    cs = begin([remote(line, line, gs2.at[n], gr2.at[n], p) for n, p in enumerate(peers_xc)])
    early_a = gram_loop(trial_rows, lambda r: [AX[r], TP[r]])
    finish_all(v3)
    listed = pltpu.make_async_copy(CI, SC, dloc.at[6])
    listed.start()
    listed.wait()
    finish_all(cs)
    ndev = ngx * ngy
    every_vals = VA.reshape(ndev, 3 * groups, groups)
    every_rhs = G0.reshape(ndev, count, groups)
    every_cols = SC.reshape(ndev, 1, LANES)
    eye = (lax.broadcasted_iota(jnp.int32, (groups, groups), 0)
           == lax.broadcasted_iota(jnp.int32, (groups, groups), 1))

    def scale(d):
        full = jnp.where(eye, every_vals[d, 0:groups, :].astype(f32), 0.0)
        return damping / jnp.sum(full, axis=0, keepdims=True)

    def columns(d):
        return [every_cols[d, 0, n] for n in (1, 2)]

    def update(d, own, others, factor):
        lhs = jnp.concatenate(split2(jnp.concatenate([own] + others, axis=1)), axis=0)
        weights = jnp.concatenate([every_vals[d, n * groups:(n + 1) * groups, :] for n in range(3)], axis=1)
        total = dot_last(lhs, weights)
        return own + factor * (every_rhs[d] - total[:count] - total[count:])

    ring1 = [me] + columns(me)
    first = [(d, scale(d)) for d in ring1]
    second = {}
    for n in (1, 2):
        for k, d in enumerate(columns(ring1[n])):
            second[(n, k)] = (d, scale(d))
    z1 = [every_rhs[d] * f for d, f in first]
    z2 = {key: every_rhs[d] * f for key, (d, f) in second.items()}
    y2 = {}
    for key, (d, f) in second.items():
        y2[key] = update(d, z2[key], [every_rhs[q] * scale(q) for q in columns(d)], f)
    y1 = [update(d, z1[n], z1[1:] if n == 0 else [z2[(n, 0)], z2[(n, 1)]], f) for n, (d, f) in enumerate(first)]
    x1 = [update(d, y1[n], y1[1:] if n == 0 else [y2[(n, 0)], y2[(n, 1)]], f) for n, (d, f) in enumerate(first)]
    e = update(me, x1[0], x1[1:], first[0][1])
    tiles = 2 * count // H

    near[4] = e
    cs = begin([remote(near.at[4], near.at[3 * s + t], as_.at[n], ar_.at[n], wrapped(1 - s, 1 - t))
                for n, (s, t) in enumerate(steps)])
    finish_all(cs)

    def spread(b, _):
        s = jnp.where(b == 0, 0, jnp.where(b == ext // H - 1, 2, 1))
        res = []
        for g in main:
            idx = coef(AGG, g, b * H).astype(jnp.int32)
            own = jnp.take_along_axis(near[3 * s + 1, g * H:(g + 1) * H, :], idx, axis=1)
            res.append(jnp.where(coef(INV, g, b * H) > 0.0, own, 0.0))
        idx = coef(AGG, ng, b * H).astype(jnp.int32)
        ev = jnp.zeros((H, LANES), f32)
        for g in main:
            lf = jnp.take_along_axis(near[3 * s, g * H:(g + 1) * H, :], idx, axis=1)
            rt = jnp.take_along_axis(near[3 * s + 2, g * H:(g + 1) * H, :], idx, axis=1)
            ev = jnp.where(win[g], jnp.where(in_a, lf, rt), ev)
        res.append(jnp.where(coef(INV, ng, b * H) > 0.0, ev, 0.0))
        put(FA, b, res)
        put(FR, b, rights(res, at_r))
        put(FL, b, lefts(res, at_l))
        return 0

    loop(ext // H, spread, 0, 6)

    def make4(r, k):
        b = r // H
        f, fr, fl = get(FA, b), get(FR, b), get(FL, b)
        up = f if k is None or k % 4 != 3 else get(FA, (r + 1) // H)
        dn = f if k is None or k % 4 != 0 else get(FA, (r - 1) // H)
        s, x = get(S, r), get(SM, r)
        d, nx = [], []
        for g in every:
            v = s[g] - f[g] + (coef(CXS, g, r) * up[g] + coef(PXS, g, r) * dn[g]
                               + coef(CYS, g, r) * fr[g] + coef(PYS, g, r) * fl[g])
            v = v * (1.0 / theta)
            d.append(v)
            nx.append(x[g] + f[g] + v)
        put(D1, r, d)
        put(SM, r, nx)
        return d

    def make5(r, k):
        d, s, x = get(D1, r), get(S, r), get(SM, r)
        d = [CHEB[0][0] * d[g] + CHEB[0][1] * s[g] for g in every]
        put(D2, r, d)
        put(SM, r, [x[g] + d[g] for g in every])
        return d

    def make6(r, k):
        d, s, x = get(D2, r), get(S, r), get(SM, r)
        return [x[g] + (CHEB[1][0] * d[g] + CHEB[1][1] * s[g]) for g in every]

    AW = B

    def fin6(r, w, t):
        for g in main:
            v = turn(w[g], -16 * g)
            xw_out[pl.ds(g * H * rows + r - H, H, rows), :] = v
            AW[r, g * H:(g + 1) * H, :] = turn(coef(DIA, g, r) * (w[g] - t[g]), -16 * g)

    march(make4, fin1, 2, ext - 4, 20)
    march(make5, fin_s, 5, rows + 4, 22)

    march(make6, fin6, 7, rows, 8)
    store = pltpu.make_async_copy(xw_out, out, dloc.at[5])
    store.start()

    def gram_late(n, total):
        halves = []
        for k in range(2):
            r = 2 * n + k
            w = [raw(xw_out, g, r, rows) for g in main]
            halves.append(jnp.concatenate(
                [raw(xr, g, r, rows) for g in main]
                + w + [raw(pr, g, r, rows) for g in main] + w + [AW[H + r, 0:count, :]], axis=0))
        both = jnp.concatenate(halves, axis=1)
        high, low = split2(both)
        lhs = jnp.concatenate([high[3 * count:], low[3 * count:]], axis=0)
        rhs_ = jnp.concatenate([high[:3 * count], low[:3 * count]], axis=0)
        return total + dot_last(lhs, rhs_)

    late = loop(rows // 2, gram_late, jnp.zeros((4 * count, 6 * count), f32), 8)

    def folded(total, width):
        total = total[:2 * count] + total[2 * count:]
        total = total[:, :width] + total[:, width:]
        return jnp.concatenate([total, jnp.zeros((2 * count, LANES - width), f32)], axis=1)

    early = jnp.concatenate([folded(early_b, 2 * count)[:, :2 * count], folded(early_a, 2 * count)[:, :LANES - 2 * count]],
                            axis=1)
    late = folded(late, 3 * count)
    for t in range(tiles):
        t1[t, 0] = early[t * H:(t + 1) * H]
        t1[t, 1] = late[t * H:(t + 1) * H]

    def each_owner(act):
        for t in range(tiles):
            @pl.when(j != t)
            def _(t=t):
                act(t)

    each_owner(lambda t: remote(t1.at[t], u1.at[j], es1.at[t], er1.at[j], (i, t)).start())

    @pl.when(j < tiles)
    def _():
        u1[j] = t1[j]
        for o in range(1, ngy):
            src = lax.rem(j + o, ngy)
            remote(t1.at[0], u1.at[src], es1.at[0], er1.at[src], (i, src)).wait_recv()
        u2[i] = summed(u1, ngy)
        cx_ = begin([remote(u2.at[i], u2.at[i], es2.at[n], er2.at[n], p) for n, p in enumerate(peers_x)])
        finish_all(cx_)
        u3[j] = summed(u2, ngx)
        for o in range(1, ngy):
            remote(u3.at[j], u3.at[j], es3.at[o], er3.at[j], (i, lax.rem(j + o, ngy))).start()
        for o in range(1, ngy):
            remote(u3.at[j], u3.at[j], es3.at[o], er3.at[j], (i, lax.rem(j + o, ngy))).wait_send()

    each_owner(lambda t: remote(t1.at[t], u1.at[j], es1.at[t], er1.at[j], (i, t)).wait_send())
    each_owner(lambda t: remote(u3.at[t], u3.at[t], es3.at[0], er3.at[t], (i, t)).wait_recv())

    E = jnp.concatenate([u3[t, 0] for t in range(tiles)], axis=0)
    L = jnp.concatenate([u3[t, 1] for t in range(tiles)], axis=0)
    k = count
    pad = jnp.zeros((LANES - 2 * k, LANES), f32)
    ET = jnp.concatenate([E, pad], axis=0).T
    LT = jnp.concatenate([L, pad], axis=0).T

    def cat(blocks):
        return jnp.concatenate([jnp.concatenate(line, axis=1) for line in blocks], axis=0)

    gb_ref[...] = cat([[E[0:k, 0:k], LT[0:k, 0:k], E[0:k, k:2 * k]],
                       [L[0:k, 0:k], L[0:k, k:2 * k], L[0:k, 2 * k:3 * k]],
                       [E[k:2 * k, 0:k], LT[2 * k:3 * k, 0:k], E[k:2 * k, k:2 * k]]])
    ga_ref[...] = cat([[E[0:k, 2 * k:3 * k], LT[0:k, k:2 * k], ET[2 * k:3 * k, k:2 * k]],
                       [L[k:2 * k, 0:k], L[k:2 * k, k:2 * k], L[k:2 * k, 2 * k:3 * k]],
                       [E[k:2 * k, 2 * k:3 * k], LT[2 * k:3 * k, k:2 * k],
                        E[k:2 * k, 3 * k:4 * k] + ET[3 * k:4 * k, k:2 * k]]])
    store.wait()
    @pl.when(exists(0, -1))
    def _():
        side_p().wait_send()
    for d in moves:
        @pl.when(exists(*d))
        def _(d=d):
            for copy in copies_of(d):
                copy.wait_send()


def per_device(eigvecs, search_dir, conduct, shift, aggregate, coarse_cols, coarse_vals):
    count, rows, width = eigvecs.shape
    groups = coarse_vals.shape[2]
    ngx, ngy = lax.axis_size("gx"), lax.axis_size("gy")
    ext = rows + 2 * H
    ng = count // H
    quarter, half = rows // 4, rows // 2
    lines = (ng + 1) * H
    tiles = 2 * count // H
    dma = pltpu.SemaphoreType.DMA
    v = pltpu.VMEM

    def fl(*shape):
        return v(shape, f32)

    scratch = [
        fl(count * rows, width), fl(count * rows, width), fl(4, ext, width),
        fl(count, H, width), fl(count, H, width), fl(count, width),
        fl(quarter, H, LANES), fl(quarter, H, LANES), fl(half, LANES),
        fl(quarter, H, LANES), fl(quarter, H, LANES), fl(half, LANES), fl(half, LANES),
        fl(H, H, LANES), fl(H, H, LANES), fl(H, H, LANES), fl(H, H, LANES),
        fl(H, LANES), fl(H, LANES), fl(H, LANES), fl(H, LANES),
        fl(ext, lines, LANES), fl(ext, lines, LANES), fl(ext, lines, LANES), fl(ext, lines, LANES),
        fl(ext, lines, LANES), fl(ext, lines, LANES),
        fl(rows, count, LANES), fl(rows, count, LANES),
        fl(7, ng + 1, ext, LANES),
        fl(ngy, H, LANES), fl(ngx, H, LANES),
        v((ngx, ngy // 2, 2, 3 * groups, groups), jnp.bfloat16),
        v((ngx, ngy // 2, 2, 1, LANES), jnp.int32), pltpu.SMEM((ngx, ngy // 2, 2, 1, LANES), jnp.int32),
        fl(ngx, ngy // 2, 2, count, groups),
        fl(rows // H, count, LANES),
        fl(9, count, groups),
        fl(ext // H + 1, lines, LANES), fl(ext // H, lines, LANES), fl(ext // H, lines, LANES),
        fl(count * rows, width), fl(tiles, 2, H, LANES),
        fl(ngy, 2, H, LANES), fl(ngx, 2, H, LANES), fl(ngy, 2, H, LANES),
        fl(count, LANES),
        dma((7,)), dma((24,)), dma((24,)),
        dma((ngy - 1,)), dma((ngy - 1,)), dma((ngx - 1,)), dma((ngx - 1,)),
        dma((ngy - 1,)), dma((ngy - 1,)), dma((2 * ngx,)), dma((2 * ngx,)),
        dma((8,)), dma((8,)),
        dma((tiles,)), dma((ngy,)), dma((ngx - 1,)), dma((ngx - 1,)), dma((ngy,)), dma((ngy,)),
        dma((ngx * ngy,)), dma((ngx * ngy,)), dma((2 * ngx,)), dma((2 * ngx,)),
        fl(rows // H, H, LANES), fl(rows // H, H, LANES), dma((2,)),
    ]
    anyspace = pl.BlockSpec(memory_space=pl.ANY)
    vmem = pl.BlockSpec(memory_space=pltpu.VMEM)
    smem = pl.BlockSpec(memory_space=pltpu.SMEM)
    size = 3 * count
    out, ga, gb = pl.pallas_call(
        functools.partial(kernel, ngx, ngy, rows),
        out_shape=[jax.ShapeDtypeStruct((count * rows, width), f32),
                   jax.ShapeDtypeStruct((size, size), f32), jax.ShapeDtypeStruct((size, size), f32)],
        in_specs=[anyspace, anyspace, anyspace, anyspace, anyspace, vmem, smem, anyspace],
        out_specs=[anyspace, vmem, vmem],
        scratch_shapes=scratch,
        compiler_params=pltpu.CompilerParams(vmem_limit_bytes=VMEM_CAP, collective_id=0, has_side_effects=True),
        name="step",
    )(eigvecs.reshape(count * rows, width), eigvecs, search_dir.reshape(count * rows, width), conduct, shift,
      aggregate, coarse_cols, coarse_vals.reshape(-1, groups))
    return out.reshape(count, rows, width), ga, gb


def solution(mesh):
    placed = (
        P(None, "gx", "gy"),
        P(None, "gx", "gy"),
        P(None, "gx", "gy"),
        P("gx", "gy"),
        P("gx", "gy"),
        P(("gx", "gy"), None),
        P(("gx", "gy"), None, None, None),
    )
    return jax.shard_map(
        per_device,
        mesh=mesh,
        in_specs=placed,
        out_specs=(P(None, "gx", "gy"), P(), P()),
        check_vma=False,
    )
```

```python
import functools

import jax
import jax.numpy as jnp
from jax import lax
from jax.experimental import pallas as pl
from jax.experimental.pallas import tpu as pltpu
from jax.sharding import PartitionSpec as P

H = 8
LANES = 128
VMEM_CAP = 60 * 1024 * 1024

cheb_lo = 0.3
cheb_hi = 2.0
damping = 0.6
theta = (cheb_hi + cheb_lo) / 2.0
delta = (cheb_hi - cheb_lo) / 2.0
sigma = theta / delta
RHO0 = 1.0 / sigma
RHO1 = 1.0 / (2.0 * sigma - RHO0)
RHO2 = 1.0 / (2.0 * sigma - RHO1)
CHEB = ((RHO1 * RHO0, 2.0 * RHO1 / delta), (RHO2 * RHO1, 2.0 * RHO2 / delta))

CONTRACT_LAST = (((1,), (1,)), ((), ()))
CXS, PXS, CYS, PYS, DIA, INV, AGG = range(7)
f32 = jnp.float32


def loop(number, body, carry, unroll):
    def several(n, carry):
        for k in range(unroll):
            carry = body(n * unroll + k, carry)
        return carry
    return lax.fori_loop(0, number // unroll, several, carry)


def split2(value):
    high = value.astype(jnp.bfloat16)
    low = (value - high.astype(f32)).astype(jnp.bfloat16)
    return high, low


def turn(value, by):
    by = by % LANES
    return pltpu.roll(value, by, 1) if by else value


def dot_last(a, b):
    return lax.dot_general(a, b, CONTRACT_LAST, preferred_element_type=f32)


def remote(src, dst, send, recv, peer):
    return pltpu.make_async_remote_copy(src_ref=src, dst_ref=dst, send_sem=send, recv_sem=recv,
                                        device_id=peer, device_id_type=pl.DeviceIdType.MESH)


def kernel(ngx, ngy, rows, x2, x3, p2, cond, shift, agg, cols, vals, out, ga_ref, gb_ref,
           xr, pr, C, top, bot, pb, toe, tow, pc, wb, eb, wc, ec, nwb, neb, swb, seb, nwc, nec, swc, sec,
           XW, B, S, D1, D2, SM, AX, TP, CO, n1, n2, VA, CI, SC, G0, RS, near, FA, FR, FL,
           xw_out, t1, u1, u2, u3, part, dloc, hs, hr, ns1, nr1, ns2, nr2, gs1, gr1, gs2, gr2, as_, ar_,
           es1, er1, es2, er2, es3, er3, vs, vr, ws, wr, tpw, tpe, ps, GT):
    count = x3.shape[0]
    ext = rows + 2 * H
    ng = count // H
    quarter = rows // 4
    i, j = lax.axis_index("gx"), lax.axis_index("gy")
    me = i * ngy + j
    nz = ngy // 2
    z, c = j // 2, lax.rem(j, 2)
    partner = (i, j + 1 - 2 * c)
    peers_z = [(i, lax.rem(z + o, nz) * 2 + c) for o in range(1, nz)]
    peers_y = [(i, lax.rem(j + o, ngy)) for o in range(1, ngy)]
    peers_x = [(lax.rem(i + o, ngx), j) for o in range(1, ngx)]
    def flipped(at, bits):
        step = 1
        while step <= bits:
            if bits & step:
                at = at + step - 2 * step * lax.rem(at // step, 2)
            step *= 2
        return at

    near_x = [m for m in range(1, ngx) if m & (m - 1) == 0]
    far_x = [m for m in range(1, ngx) if m & (m - 1)]
    peers_xc = [(ii, j) for ii, _ in peers_x] + [partner] + [(ii, partner[1]) for ii, _ in peers_x]
    steps = [(s, t) for s in range(3) for t in range(3) if (s, t) != (1, 1)]

    def wrapped(dx, dy):
        return (lax.rem(i + dx + ngx, ngx), lax.rem(j + dy + ngy, ngy))

    lane = lax.broadcasted_iota(jnp.int32, (H, LANES), 1)
    LL = lax.rem(lane + H, LANES)
    in_a = lax.rem(LL, 16) < 8
    win = [LL // 16 == g for g in range(ng)]
    in_win = LL < 16 * ng
    at_r = [lane == (16 * g - 1) % LANES for g in range(ng)]
    at_l = [lane == 16 * g for g in range(ng)]

    def begin(copies):
        for copy in copies:
            copy.start()
        return copies

    def finish_all(copies):
        for copy in copies:
            copy.wait()

    local = [pltpu.make_async_copy(x2, xr, dloc.at[0]), pltpu.make_async_copy(p2, pr, dloc.at[1]),
             pltpu.make_async_copy(cond, C.at[0:2, H:H + rows], dloc.at[2]),
             pltpu.make_async_copy(shift, C.at[2, H:H + rows], dloc.at[3]),
             pltpu.make_async_copy(vals, VA.at[i, z, c], dloc.at[4])]
    for copy in local:
        copy.start()

    diagonal = [wrapped(dx, dy) for dx in (-1, 1) for dy in (-1, 1)]
    greeted = peers_y + peers_x + diagonal + [(ii, partner[1]) for ii, _ in peers_x]
    barrier = pltpu.get_barrier_semaphore()
    for peer in greeted:
        pl.semaphore_signal(barrier, inc=1, device_id=peer, device_id_type=pl.DeviceIdType.MESH)

    expand = jnp.where(lax.broadcasted_iota(jnp.int32, (agg.shape[1], LANES), 1) // H
                       == lax.broadcasted_iota(jnp.int32, (agg.shape[1], LANES), 0), 1.0, 0.0).astype(jnp.bfloat16)
    ids = jnp.dot(agg[...].astype(f32).astype(jnp.bfloat16), expand, preferred_element_type=f32)
    for b in range(rows // H):
        C[3, H + b * H:2 * H + b * H, :] = jnp.broadcast_to(ids[b:b + 1, :], (H, LANES))

    def raw(ref, g, r, stride):
        return ref[pl.ds(g * H * stride + r, H, stride), :]

    local[0].wait()
    local[1].wait()

    def pack(r, _):
        east = west = None
        for q in reversed(range(4)):
            row = q * quarter + r
            m = [turn(raw(xr, g, row, rows), 16 * g) for g in range(ng)]
            for g in range(ng):
                XW[H + row, g * H:(g + 1) * H, :] = m[g]
            both = m[ng - 1]
            for g in range(ng - 1):
                both = jnp.where(win[g], m[g], both)
            fe = turn(both, H * (q % 2) + 48 * (q // 2))
            fw = turn(both, -H * (q % 2) + 48 * (q // 2))
            if q == 3:
                east, west = fe, fw
            else:
                low = (LL < 48) if q < 2 else (LL < 96)
                ea = in_a if q % 2 == 0 else ~in_a
                wa = ~in_a if q % 2 == 0 else in_a
                east = jnp.where(low & ea, fe, east)
                west = jnp.where(low & wa, fw, west)
        toe[r] = east
        tow[r] = west
        return 0

    loop(quarter, pack, 0, 4)
    for g in range(ng):
        part[g * H:(g + 1) * H, :] = raw(pr, g, 0, rows)
    local[2].wait()
    local[3].wait()
    half = rows // 2
    lane_h = lax.broadcasted_iota(jnp.int32, (half, LANES), 1)
    LLh = lax.rem(lane_h + H, LANES)

    def coef_pack(lo):
        total = C[3, H + lo:H + lo + half, :]
        total = turn(total, 48)
        for n in range(3):
            total = jnp.where(LLh // 16 == n, turn(C[n, H + lo:H + lo + half, :], 16 * n), total)
        return total

    pc[...] = jnp.where(LLh < 64, coef_pack(0), turn(coef_pack(half), 64))
    def gram_loop(make_lhs, make_rhs):
        def body(n, total):
            lhs = jnp.concatenate([jnp.concatenate(make_lhs(2 * n + k), axis=0) for k in range(2)], axis=1)
            rhs = lhs if make_rhs is None else jnp.concatenate(
                [jnp.concatenate(make_rhs(2 * n + k), axis=0) for k in range(2)], axis=1)
            lh = jnp.concatenate(split2(lhs), axis=0)
            return total + dot_last(lh, lh if make_rhs is None else jnp.concatenate(split2(rhs), axis=0))
        return loop(rows // 2, body, jnp.zeros((4 * count, 4 * count), f32), 8)

    def trial_rows(r):
        return [raw(xr, g, r, rows) for g in range(ng)] + [raw(pr, g, r, rows) for g in range(ng)]

    pl.semaphore_wait(barrier, len(greeted))

    last = quarter - H
    moves = {
        (-1, 0): [(x3.at[:, 0:H], bot), (C.at[:, H:2 * H], C.at[:, H + rows:ext]), (part, pb)],
        (1, 0): [(x3.at[:, rows - H:rows], top), (C.at[:, rows:rows + H], C.at[:, 0:H])],
        (0, 1): [(toe, wb), (pc, wc)],
        (0, -1): [(tow, eb), (pc, ec)],
        (-1, 1): [(toe.at[0:H], swb), (pc.at[0:H], swc)],
        (-1, -1): [(tow.at[0:H], seb), (pc.at[0:H], sec)],
        (1, 1): [(toe.at[last:quarter], nwb), (pc.at[half - H:half], nwc)],
        (1, -1): [(tow.at[last:quarter], neb), (pc.at[half - H:half], nec)],
    }

    def exists(dx, dy):
        return (i + dx >= 0) & (i + dx < ngx) & (j + dy >= 0) & (j + dy < ngy)

    def copies_of(d):
        base = 3 * list(moves).index(d)
        return [remote(src, dst, hs.at[base + n], hr.at[base + n], (i + d[0], j + d[1]))
                for n, (src, dst) in enumerate(moves[d])]

    for d in moves:
        @pl.when(exists(*d))
        def _(d=d):
            for copy in copies_of(d):
                copy.start()

        @pl.when(jnp.logical_not(exists(-d[0], -d[1])))
        def _(d=d):
            for _, dst in moves[d]:
                dst[...] = jnp.zeros(dst.shape, dst.dtype)

    mine = lax.broadcasted_iota(jnp.int32, (1, LANES), 1)
    CI[i, z, c] = jnp.where(mine == 0, cols[0, 0], jnp.where(mine == 1, cols[0, 1], cols[0, 2]))
    local[4].wait()
    v1 = []
    for n, p in enumerate(peers_z):
        v1.append(remote(VA.at[i, z, c], VA.at[i, z, c], vs.at[2 * n], vr.at[2 * n], p))
        v1.append(remote(CI.at[i, z, c], CI.at[i, z, c], vs.at[2 * n + 1], vr.at[2 * n + 1], p))
    begin(v1)
    nvs = 2 * (nz - 1)

    def block_pair(column, row, at, peer):
        return [remote(VA.at[column, row, c], VA.at[column, row, c], vs.at[at], vr.at[at], peer),
                remote(CI.at[column, row, c], CI.at[column, row, c], vs.at[at + 1], vr.at[at + 1], peer)]

    v2 = []
    for m in range(1, ngx):
        v2.append(begin(block_pair(i, z, nvs + 2 * (m - 1), (flipped(i, m), j))))

    for ref in (S, B):
        for row in (0, 1, ext - 2, ext - 1):
            ref[row] = jnp.zeros(ref.shape[1:], f32)

    def pack_p(r, _):
        west = jnp.zeros((H, LANES), f32)
        for q in range(H):
            for g in range(ng):
                to = ng * q + g
                west = jnp.where(lane == to, turn(raw(pr, g, q * (rows // H) + r, rows), to), west)
        tpw[r] = west
        return 0

    loop(rows // H, pack_p, 0, 2)

    def side_p():
        return remote(tpw, tpe, ps.at[0], ps.at[1], (i, j - 1))

    @pl.when(exists(0, -1))
    def _():
        side_p().start()

    @pl.when(jnp.logical_not(exists(0, 1)))
    def _():
        tpe[...] = jnp.zeros(tpe.shape, f32)

    early_b = gram_loop(trial_rows, None)
    for d in moves:
        @pl.when(exists(-d[0], -d[1]))
        def _(d=d):
            for copy in copies_of(d):
                copy.wait_recv()

    for ref, at in ((top, 0), (bot, H + rows)):
        flat = ref.reshape(count * H, LANES)
        for r in range(H):
            for g in range(ng):
                XW[at + r, g * H:(g + 1) * H, :] = turn(raw(flat, g, r, H), 16 * g)

    def edge(w, e, q):
        w = turn(w, -(H * (q % 2) + 48 * (q // 2)))
        e = turn(e, H * (q % 2) - 48 * (q // 2))
        return jnp.where(in_win, jnp.where(in_a, w, e), 0.0)

    at_e = slice(ng * H, (ng + 1) * H)

    def unpack(r, _):
        for q in range(4):
            XW[H + q * quarter + r, at_e, :] = edge(wb[r], eb[r], q)
        return 0

    loop(quarter, unpack, 0, 8)
    for r in range(H):
        XW[r, at_e, :] = edge(nwb[r], neb[r], 3)
        XW[H + rows + r, at_e, :] = edge(swb[r], seb[r], 0)

    def masks(number):
        ln = lax.broadcasted_iota(jnp.int32, (number, LANES), 1)
        return ln, lax.rem(ln + H, LANES)

    def joined(w, e):
        _, l2 = masks(w.shape[0])
        return jnp.where(lax.rem(l2, 16) < 8, w, e)

    side = joined(wc[...], ec[...])
    wide = jnp.concatenate([turn(joined(nwc[...], nec[...]), 64), side, turn(side, 64),
                            joined(swc[...], sec[...])], axis=0)
    lnx, llx = masks(ext)

    def fields(n):
        m = C[n]
        res = [turn(m, 16 * g) for g in range(ng)]
        e = jnp.zeros_like(wide)
        for g in range(ng):
            e = jnp.where(llx // 16 == g, turn(wide, 16 * (g - n)), e)
        return res + [e]

    def lefts(v, ml):
        l = [turn(a, 1) for a in v]
        e = l[ng]
        for g in range(ng):
            e = jnp.where(ml[g], l[g], e)
        return [jnp.where(ml[g], l[ng], l[g]) for g in range(ng)] + [e]

    def rights(v, mr):
        l = [turn(a, LANES - 1) for a in v]
        e = l[ng]
        for g in range(ng):
            e = jnp.where(mr[g], l[g], e)
        return [jnp.where(mr[g], l[ng], l[g]) for g in range(ng)] + [e]

    cx, cy, sh, ag = fields(0), fields(1), fields(2), fields(3)
    mlx = [lnx == 16 * g for g in range(ng)]
    py = lefts(cy, mlx)
    for g in range(ng + 1):
        px = pltpu.roll(cx[g], 1, 0)
        diag = cx[g] + px + cy[g] + py[g] + sh[g]
        inside = sh[g] > 0.0
        inv = jnp.where(inside, 1.0 / jnp.where(inside, diag, 1.0), 0.0)
        CO[CXS, g] = inv * cx[g]
        CO[PXS, g] = inv * px
        CO[CYS, g] = inv * cy[g]
        CO[PYS, g] = inv * py[g]
        CO[DIA, g] = diag
        CO[INV, g] = inv
        CO[AGG, g] = ag[g]

    def coef(n, g, r):
        return jnp.broadcast_to(CO[n, g, pl.ds(r, 1), :], (H, LANES))

    every = range(ng + 1)
    main = range(ng)

    def get(ref, r, groups=every):
        return [ref[r, g * H:(g + 1) * H, :] for g in groups]

    def put(ref, r, v):
        for g, a in enumerate(v):
            ref[r, g * H:(g + 1) * H, :] = a

    def spreadout(r, vm, vc, vp):
        rt, lf = rights(vc, at_r), lefts(vc, at_l)
        return [coef(CXS, g, r) * vp[g] + coef(PXS, g, r) * vm[g]
                + coef(CYS, g, r) * rt[g] + coef(PYS, g, r) * lf[g] for g in every]

    def march(make, finish, first, number, unroll, after=None):
        def body(n, carry):
            vm, vc = carry
            for k in range(unroll):
                r = first + 1 + n * unroll + k
                vp = make(r + 1, k)
                finish(r, vc, spreadout(r, vm, vc, vp))
                vm, vc = vc, vp
            if after is not None:
                after(first + 1 + n * unroll - H)
            return vm, vc
        lax.fori_loop(0, number // unroll, body, (make(first, None), make(first + 1, None)))

    def fin_image(r, vc, t):
        put(B, r, [vc[g] - t[g] for g in every])

    march(lambda r, k: get(XW, r), fin_image, 1, ext - 4, 20)

    def ratio(n, carry):
        num, den = carry
        num, den = list(num), list(den)
        for k in range(4):
            r = H + n * 4 + k
            for g in main:
                xv = XW[r, g * H:(g + 1) * H, :]
                num[g] = num[g] + xv * (coef(DIA, g, r) * B[r, g * H:(g + 1) * H, :])
                den[g] = den[g] + xv * xv
        return tuple(num), tuple(den)

    zero = jnp.zeros((H, LANES), f32)
    num, den = loop(rows // 4, ratio, ((zero,) * ng, (zero,) * ng), 4)
    nd = zero
    for g in main:
        nd = jnp.where(lane == 2 * g, jnp.sum(num[g], axis=1, keepdims=True), nd)
        nd = jnp.where(lane == 2 * g + 1, jnp.sum(den[g], axis=1, keepdims=True), nd)

    def summed(slots, number):
        total = slots[0]
        for n in range(1, number):
            total = total + slots[n]
        return total

    n1[j] = nd
    c1 = begin([remote(n1.at[j], n1.at[j], ns1.at[n], nr1.at[n], p) for n, p in enumerate(peers_y)])

    def forward(r, _):
        for q in range(H):
            row = q * (rows // H) + r
            for g in main:
                pv = raw(pr, g, row, rows)
                nxt = turn(tpe[r], LANES - 1 - (ng * q + g))
                rt = jnp.where(lane == LANES - 1, nxt, turn(pv, LANES - 1))
                below = raw(pr, g, jnp.minimum(row + 1, rows - 1), rows)
                below = jnp.where(row == rows - 1, pb[g * H:(g + 1) * H, :], below)
                TP[row, g * H:(g + 1) * H, :] = coef(DIA, 0, H + row) * (
                    0.5 * pv - coef(CXS, 0, H + row) * below - coef(CYS, 0, H + row) * rt)
        return 0

    finish_all(c1)
    n2[i] = summed(n1, ngy)
    c1 = begin([remote(n2.at[i], n2.at[i], ns2.at[n], nr2.at[n], p) for n, p in enumerate(peers_x)])

    finish_all(v1)
    for pair in v2:
        finish_all(pair)
    v2 = {m: [] for m in range(1, ngx)}
    for o in range(1, nz):
        zo = lax.rem(z + o, nz)
        for m in near_x:
            v2[m] += begin(block_pair(i, zo, nvs + 2 * (o * (ngx - 1) + m - 1), (flipped(i, m), j)))
        for m in far_x:
            v2[m] += begin(block_pair(flipped(i, m), z, nvs + 2 * (o * (ngx - 1) + m - 1), (i, zo * 2 + c)))
    v3 = begin([remote(VA.at[i, :, c], VA.at[i, :, c], ws.at[0], wr.at[0], partner),
                remote(CI.at[i, :, c], CI.at[i, :, c], ws.at[1], wr.at[1], partner)])

    def image_rows(n, _):
        for k in range(4):
            r = n * 4 + k
            for g in main:
                AX[r, g * H:(g + 1) * H, :] = turn(
                    coef(DIA, g, H + r) * B[H + r, g * H:(g + 1) * H, :], -16 * g)
        return 0

    finish_all(c1)
    nd = summed(n2, ngx)
    lam = []
    for g in main:
        a = jnp.sum(jnp.where(lane == 2 * g, nd, 0.0), axis=1, keepdims=True)
        b = jnp.sum(jnp.where(lane == 2 * g + 1, nd, 0.0), axis=1, keepdims=True)
        lam.append(jnp.broadcast_to(a / b, (H, LANES)))
    lam_e = lam[ng - 1]
    for g in range(ng - 1):
        lam_e = jnp.where(win[g], lam[g], lam_e)
    lam = lam + [lam_e]

    def make1(r, k):
        b, xv = get(B, r), get(XW, r)
        d = [(b[g] - lam[g] * (coef(INV, g, r) * xv[g])) * (1.0 / theta) for g in every]
        put(D1, r, d)
        return d

    def fin1(r, d, t):
        put(S, r, [(theta - 1.0) * d[g] + t[g] for g in every])

    def make2(r, k):
        d, s = get(D1, r), get(S, r)
        d = [CHEB[0][0] * d[g] + CHEB[0][1] * s[g] for g in every]
        put(D2, r, d)
        return d

    def fin_s(r, d, t):
        s = get(S, r)
        put(S, r, [s[g] - d[g] + t[g] for g in every])

    def make3(r, k):
        d1, d2, s = get(D1, r), get(D2, r), get(S, r)
        d = [CHEB[1][0] * d2[g] + CHEB[1][1] * s[g] for g in every]
        put(SM, r, [d1[g] + d2[g] + d[g] for g in every])
        return d

    march(make1, fin1, 1, ext - 4, 20)
    march(make2, fin_s, 1, ext - 4, 20)
    march(make3, fin_s, 1, ext - 4, 20)

    groups = near.shape[2]
    per = 2
    ids_t = lax.broadcasted_iota(jnp.int32, (groups, LANES), 0)

    def block_sum(b, _):
        for g in main:
            total = None
            for k in range(H):
                r = H + b * H + k
                term = coef(DIA, g, r) * S[r, g * H:(g + 1) * H, :]
                total = term if total is None else total + term
            RS[b, g * H:(g + 1) * H, :] = turn(total, -16 * g)
        return 0

    loop(rows // H, block_sum, 0, 4)

    def gathered(b, total):
        parts, hots = [], []
        for k in range(per):
            parts.append(RS[b * per + k])
            own = CO[AGG, 0, pl.ds(H + (b * per + k) * H, 1), :].astype(jnp.int32)
            hots.append(jnp.where(ids_t == own, 1.0, 0.0).astype(jnp.bfloat16))
        high, low = split2(jnp.concatenate(parts, axis=1))
        return total + dot_last(jnp.concatenate([high, low], axis=0), jnp.concatenate(hots, axis=1))

    total = loop(rows // H // per, gathered, jnp.zeros((2 * count, groups), f32), 8)
    rhs = total[:count] + total[count:]

    own_rhs = G0.at[i, z, c]
    own_rhs[...] = rhs
    cs = begin([remote(own_rhs, own_rhs, gs1.at[n], gr1.at[n], p) for n, p in enumerate(peers_z)])
    loop(rows // 4, image_rows, 0, 4)
    @pl.when(exists(0, 1))
    def _():
        side_p().wait_recv()
    loop(rows // 8, forward, 0, 2)
    for n, m in enumerate(near_x + far_x):
        finish_all(v2[m])
        at = flipped(i, m)
        v3 += begin([remote(VA.at[at, :, c], VA.at[at, :, c], ws.at[2 * n + 2], wr.at[2 * n + 2], partner),
                     remote(CI.at[at, :, c], CI.at[at, :, c], ws.at[2 * n + 3], wr.at[2 * n + 3], partner)])
    finish_all(cs)
    line = G0.at[i, :, c]
    cs = begin([remote(line, line, gs2.at[n], gr2.at[n], p) for n, p in enumerate(peers_xc)])
    early_a = gram_loop(trial_rows, lambda r: [AX[r], TP[r]])
    finish_all(v3)
    listed = pltpu.make_async_copy(CI, SC, dloc.at[6])
    listed.start()
    listed.wait()
    finish_all(cs)
    ndev = ngx * ngy
    every_vals = VA.reshape(ndev, 3 * groups, groups)
    every_rhs = G0.reshape(ndev, count, groups)
    every_cols = SC.reshape(ndev, 1, LANES)
    eye = (lax.broadcasted_iota(jnp.int32, (groups, groups), 0)
           == lax.broadcasted_iota(jnp.int32, (groups, groups), 1))

    def scale(d):
        full = jnp.where(eye, every_vals[d, 0:groups, :].astype(f32), 0.0)
        return damping / jnp.sum(full, axis=0, keepdims=True)

    def columns(d):
        return [every_cols[d, 0, n] for n in (1, 2)]

    def update(d, own, others, factor):
        lhs = jnp.concatenate(split2(jnp.concatenate([own] + others, axis=1)), axis=0)
        weights = jnp.concatenate([every_vals[d, n * groups:(n + 1) * groups, :] for n in range(3)], axis=1)
        total = dot_last(lhs, weights)
        return own + factor * (every_rhs[d] - total[:count] - total[count:])

    ring1 = [me] + columns(me)
    first = [(d, scale(d)) for d in ring1]
    second = {}
    for n in (1, 2):
        for k, d in enumerate(columns(ring1[n])):
            second[(n, k)] = (d, scale(d))
    z1 = [every_rhs[d] * f for d, f in first]
    z2 = {key: every_rhs[d] * f for key, (d, f) in second.items()}
    y2 = {}
    for key, (d, f) in second.items():
        y2[key] = update(d, z2[key], [every_rhs[q] * scale(q) for q in columns(d)], f)
    y1 = [update(d, z1[n], z1[1:] if n == 0 else [z2[(n, 0)], z2[(n, 1)]], f) for n, (d, f) in enumerate(first)]
    x1 = [update(d, y1[n], y1[1:] if n == 0 else [y2[(n, 0)], y2[(n, 1)]], f) for n, (d, f) in enumerate(first)]
    e = update(me, x1[0], x1[1:], first[0][1])
    tiles = 2 * count // H

    near[4] = e
    cs = begin([remote(near.at[4], near.at[3 * s + t], as_.at[n], ar_.at[n], wrapped(1 - s, 1 - t))
                for n, (s, t) in enumerate(steps)])
    finish_all(cs)

    def spread(b, _):
        s = jnp.where(b == 0, 0, jnp.where(b == ext // H - 1, 2, 1))
        res = []
        for g in main:
            idx = coef(AGG, g, b * H).astype(jnp.int32)
            own = jnp.take_along_axis(near[3 * s + 1, g * H:(g + 1) * H, :], idx, axis=1)
            res.append(jnp.where(coef(INV, g, b * H) > 0.0, own, 0.0))
        idx = coef(AGG, ng, b * H).astype(jnp.int32)
        ev = jnp.zeros((H, LANES), f32)
        for g in main:
            lf = jnp.take_along_axis(near[3 * s, g * H:(g + 1) * H, :], idx, axis=1)
            rt = jnp.take_along_axis(near[3 * s + 2, g * H:(g + 1) * H, :], idx, axis=1)
            ev = jnp.where(win[g], jnp.where(in_a, lf, rt), ev)
        res.append(jnp.where(coef(INV, ng, b * H) > 0.0, ev, 0.0))
        put(FA, b, res)
        put(FR, b, rights(res, at_r))
        put(FL, b, lefts(res, at_l))
        return 0

    loop(ext // H, spread, 0, 6)

    def make4(r, k):
        b = r // H
        f, fr, fl = get(FA, b), get(FR, b), get(FL, b)
        up = f if k is None or k % 4 != 3 else get(FA, (r + 1) // H)
        dn = f if k is None or k % 4 != 0 else get(FA, (r - 1) // H)
        s, x = get(S, r), get(SM, r)
        d, nx = [], []
        for g in every:
            v = s[g] - f[g] + (coef(CXS, g, r) * up[g] + coef(PXS, g, r) * dn[g]
                               + coef(CYS, g, r) * fr[g] + coef(PYS, g, r) * fl[g])
            v = v * (1.0 / theta)
            d.append(v)
            nx.append(x[g] + f[g] + v)
        put(D1, r, d)
        put(SM, r, nx)
        return d

    def make5(r, k):
        d, s, x = get(D1, r), get(S, r), get(SM, r)
        d = [CHEB[0][0] * d[g] + CHEB[0][1] * s[g] for g in every]
        put(D2, r, d)
        put(SM, r, [x[g] + d[g] for g in every])
        return d

    def make6(r, k):
        d, s, x = get(D2, r), get(S, r), get(SM, r)
        return [x[g] + (CHEB[1][0] * d[g] + CHEB[1][1] * s[g]) for g in every]

    AW = B

    recent = []

    def fin6(r, w, t):
        ws_, aws = [], []
        for g in main:
            v = turn(w[g], -16 * g)
            xw_out[pl.ds(g * H * rows + r - H, H, rows), :] = v
            ws_.append(v)
            aws.append(turn(coef(DIA, g, r) * (w[g] - t[g]), -16 * g))
        recent.append((ws_, aws))

    def gram_late(at):
        total = None
        for k in range(0, len(recent), 2):
            halves = []
            for m in range(2):
                w, aw = recent[k + m]
                r = at + k + m
                halves.append(jnp.concatenate([raw(xr, g, r, rows) for g in main] + w
                                              + [raw(pr, g, r, rows) for g in main] + w + aw, axis=0))
            both = jnp.concatenate(halves, axis=1)
            lhs = jnp.concatenate(split2(both[3 * count:]), axis=0)
            part_ = dot_last(lhs, jnp.concatenate(split2(both[:3 * count]), axis=0))
            total = part_ if total is None else total + part_
        del recent[:]
        GT[...] += total

    GT[...] = jnp.zeros(GT.shape, f32)
    march(make4, fin1, 2, ext - 4, 20)
    march(make5, fin_s, 5, rows + 4, 22)

    march(make6, fin6, 7, rows, 16, gram_late)
    store = pltpu.make_async_copy(xw_out, out, dloc.at[5])
    store.start()

    late = GT[...]

    def folded(total, width):
        total = total[:2 * count] + total[2 * count:]
        total = total[:, :width] + total[:, width:]
        return jnp.concatenate([total, jnp.zeros((2 * count, LANES - width), f32)], axis=1)

    early = jnp.concatenate([folded(early_b, 2 * count)[:, :2 * count], folded(early_a, 2 * count)[:, :LANES - 2 * count]],
                            axis=1)
    late = folded(late, 3 * count)
    for t in range(tiles):
        t1[t, 0] = early[t * H:(t + 1) * H]
        t1[t, 1] = late[t * H:(t + 1) * H]

    def each_owner(act):
        for t in range(tiles):
            @pl.when(j != t)
            def _(t=t):
                act(t)

    each_owner(lambda t: remote(t1.at[t], u1.at[j], es1.at[t], er1.at[j], (i, t)).start())

    @pl.when(j < tiles)
    def _():
        u1[j] = t1[j]
        for o in range(1, ngy):
            src = lax.rem(j + o, ngy)
            remote(t1.at[0], u1.at[src], es1.at[0], er1.at[src], (i, src)).wait_recv()
        u2[i] = summed(u1, ngy)
        cx_ = begin([remote(u2.at[i], u2.at[i], es2.at[n], er2.at[n], p) for n, p in enumerate(peers_x)])
        finish_all(cx_)
        u3[j] = summed(u2, ngx)
        for o in range(1, ngy):
            remote(u3.at[j], u3.at[j], es3.at[o], er3.at[j], (i, lax.rem(j + o, ngy))).start()
        for o in range(1, ngy):
            remote(u3.at[j], u3.at[j], es3.at[o], er3.at[j], (i, lax.rem(j + o, ngy))).wait_send()

    each_owner(lambda t: remote(t1.at[t], u1.at[j], es1.at[t], er1.at[j], (i, t)).wait_send())
    each_owner(lambda t: remote(u3.at[t], u3.at[t], es3.at[0], er3.at[t], (i, t)).wait_recv())

    E = jnp.concatenate([u3[t, 0] for t in range(tiles)], axis=0)
    L = jnp.concatenate([u3[t, 1] for t in range(tiles)], axis=0)
    k = count
    pad = jnp.zeros((LANES - 2 * k, LANES), f32)
    ET = jnp.concatenate([E, pad], axis=0).T
    LT = jnp.concatenate([L, pad], axis=0).T

    def cat(blocks):
        return jnp.concatenate([jnp.concatenate(line, axis=1) for line in blocks], axis=0)

    gb_ref[...] = cat([[E[0:k, 0:k], LT[0:k, 0:k], E[0:k, k:2 * k]],
                       [L[0:k, 0:k], L[0:k, k:2 * k], L[0:k, 2 * k:3 * k]],
                       [E[k:2 * k, 0:k], LT[2 * k:3 * k, 0:k], E[k:2 * k, k:2 * k]]])
    ga_ref[...] = cat([[E[0:k, 2 * k:3 * k], LT[0:k, k:2 * k], ET[2 * k:3 * k, k:2 * k]],
                       [L[k:2 * k, 0:k], L[k:2 * k, k:2 * k], L[k:2 * k, 2 * k:3 * k]],
                       [E[k:2 * k, 2 * k:3 * k], LT[2 * k:3 * k, k:2 * k],
                        E[k:2 * k, 3 * k:4 * k] + ET[3 * k:4 * k, k:2 * k]]])
    store.wait()
    @pl.when(exists(0, -1))
    def _():
        side_p().wait_send()
    for d in moves:
        @pl.when(exists(*d))
        def _(d=d):
            for copy in copies_of(d):
                copy.wait_send()


def per_device(eigvecs, search_dir, conduct, shift, aggregate, coarse_cols, coarse_vals):
    count, rows, width = eigvecs.shape
    groups = coarse_vals.shape[2]
    ngx, ngy = lax.axis_size("gx"), lax.axis_size("gy")
    ext = rows + 2 * H
    ng = count // H
    quarter, half = rows // 4, rows // 2
    lines = (ng + 1) * H
    tiles = 2 * count // H
    dma = pltpu.SemaphoreType.DMA
    v = pltpu.VMEM

    def fl(*shape):
        return v(shape, f32)

    scratch = [
        fl(count * rows, width), fl(count * rows, width), fl(4, ext, width),
        fl(count, H, width), fl(count, H, width), fl(count, width),
        fl(quarter, H, LANES), fl(quarter, H, LANES), fl(half, LANES),
        fl(quarter, H, LANES), fl(quarter, H, LANES), fl(half, LANES), fl(half, LANES),
        fl(H, H, LANES), fl(H, H, LANES), fl(H, H, LANES), fl(H, H, LANES),
        fl(H, LANES), fl(H, LANES), fl(H, LANES), fl(H, LANES),
        fl(ext, lines, LANES), fl(ext, lines, LANES), fl(ext, lines, LANES), fl(ext, lines, LANES),
        fl(ext, lines, LANES), fl(ext, lines, LANES),
        fl(rows, count, LANES), fl(rows, count, LANES),
        fl(7, ng + 1, ext, LANES),
        fl(ngy, H, LANES), fl(ngx, H, LANES),
        v((ngx, ngy // 2, 2, 3 * groups, groups), jnp.bfloat16),
        v((ngx, ngy // 2, 2, 1, LANES), jnp.int32), pltpu.SMEM((ngx, ngy // 2, 2, 1, LANES), jnp.int32),
        fl(ngx, ngy // 2, 2, count, groups),
        fl(rows // H, count, LANES),
        fl(9, count, groups),
        fl(ext // H + 1, lines, LANES), fl(ext // H, lines, LANES), fl(ext // H, lines, LANES),
        fl(count * rows, width), fl(tiles, 2, H, LANES),
        fl(ngy, 2, H, LANES), fl(ngx, 2, H, LANES), fl(ngy, 2, H, LANES),
        fl(count, LANES),
        dma((7,)), dma((24,)), dma((24,)),
        dma((ngy - 1,)), dma((ngy - 1,)), dma((ngx - 1,)), dma((ngx - 1,)),
        dma((ngy - 1,)), dma((ngy - 1,)), dma((2 * ngx,)), dma((2 * ngx,)),
        dma((8,)), dma((8,)),
        dma((tiles,)), dma((ngy,)), dma((ngx - 1,)), dma((ngx - 1,)), dma((ngy,)), dma((ngy,)),
        dma((ngx * ngy,)), dma((ngx * ngy,)), dma((2 * ngx,)), dma((2 * ngx,)),
        fl(rows // H, H, LANES), fl(rows // H, H, LANES), dma((2,)), fl(4 * count, 6 * count),
    ]
    anyspace = pl.BlockSpec(memory_space=pl.ANY)
    vmem = pl.BlockSpec(memory_space=pltpu.VMEM)
    smem = pl.BlockSpec(memory_space=pltpu.SMEM)
    size = 3 * count
    out, ga, gb = pl.pallas_call(
        functools.partial(kernel, ngx, ngy, rows),
        out_shape=[jax.ShapeDtypeStruct((count * rows, width), f32),
                   jax.ShapeDtypeStruct((size, size), f32), jax.ShapeDtypeStruct((size, size), f32)],
        in_specs=[anyspace, anyspace, anyspace, anyspace, anyspace, vmem, smem, anyspace],
        out_specs=[anyspace, vmem, vmem],
        scratch_shapes=scratch,
        compiler_params=pltpu.CompilerParams(vmem_limit_bytes=VMEM_CAP, collective_id=0, has_side_effects=True),
        name="step",
    )(eigvecs.reshape(count * rows, width), eigvecs, search_dir.reshape(count * rows, width), conduct, shift,
      aggregate, coarse_cols, coarse_vals.reshape(-1, groups))
    def last(a, b, c, x, y, z, buf, sems):
        part = a.shape[0] // 4
        ins = [pltpu.make_async_copy(a.at[pl.ds(n * part, part)], buf.at[pl.ds(n * part, part)], sems.at[n]) for n in range(4)]
        outs = [pltpu.make_async_copy(buf.at[pl.ds(n * part, part)], x.at[pl.ds(n * part, part)], sems.at[4 + n]) for n in range(4)]
        for copy in ins:
            copy.start()
        y[...] = b[...]
        z[...] = c[...]
        for u, v in zip(ins, outs):
            u.wait()
            v.start()
        for v in outs:
            v.wait()

    out, ga, gb = pl.pallas_call(
        last, out_shape=[jax.ShapeDtypeStruct(v.shape, f32) for v in (out, ga, gb)],
        in_specs=[anyspace, vmem, vmem], out_specs=[anyspace, vmem, vmem],
        scratch_shapes=[pltpu.VMEM(out.shape, f32), dma((8,))],
        compiler_params=pltpu.CompilerParams(vmem_limit_bytes=VMEM_CAP), name="last")(out, ga, gb)
    return out.reshape(count, rows, width), ga, gb


def solution(mesh):
    placed = (
        P(None, "gx", "gy"),
        P(None, "gx", "gy"),
        P(None, "gx", "gy"),
        P("gx", "gy"),
        P("gx", "gy"),
        P(("gx", "gy"), None),
        P(("gx", "gy"), None, None, None),
    )
    return jax.shard_map(
        per_device,
        mesh=mesh,
        in_specs=placed,
        out_specs=(P(None, "gx", "gy"), P(), P()),
        check_vma=False,
    )
```
